768 devices in a mesh: elem: 192 (over z, y_lo, x), band: 4 (over y_hi, core).
Axes of the slice: x: 4, y: 8 (y_hi: 2, y_lo: 4; y = y_hi * 4 + y_lo), z: 12, core: 2. Of those that a mesh axis runs over, the one named last changes fastest.
Arguments:
- orbitals: bfloat16 [24576, 2, 1536], P('elem', None, 'band'), may hold values from -6 to 6
- elem_count: int32 [192], P('elem'), may hold values from 1 to 4, as said below
- connectivity: int32 [192, 4, 343], P('elem'), may hold values from 0 to 383
- elem_coef: float32 [192, 4], P('elem'), may hold values from 0.5 to 2
- elem_matrix: bfloat16 [343, 343], replicated, may hold values from -1 to 1, as said below
- potential: float32 [24576], P('elem'), may hold values from -1 to 1
- absorber: float32 [24576], P('elem'), may hold values from 0.05 to 1
- rotation: bfloat16 [1536, 2, 512], replicated, may hold values from -0.109375 to 0.109375
Outputs:
- filtered: bfloat16 [24576, 2, 1536], P('elem', None, 'band')
- rotated: bfloat16 [24576, 2, 512], P('elem', None, 'band')
- intersection: float32 [1536, 2, 512], P('band')
The draws below stay inside these ranges and needn't reach their ends.
Inputs may be any that keep to these rules, and one draw needn't show every extreme that they name: Each block has between 1 and 4 live elements; the first elem_count[b] slots are live. `connectivity`: indices 0 to 127 name the previous block's last owned nodes, 128 to 255 the block's own nodes, the rest the next block's first nodes. `elem_matrix`: symmetric.
All inputs are finite; a program needn't handle non-finite values.
Results may differ from the reference program's by a relative error of at most 0.0055.
Values may be sent and summed in bfloat16 or wider, within the bound.
A program may use at most 32 MiB of HBM per device.

```python
import math
import jax
import jax.numpy as jnp
from jax import lax

ELEM_NODES = 343
BANDS = 1536
PANEL = 512
NODE_DEV = 128
FACE = 128
E_CAP = 4
BLOCKS = 192
NODES = 24576


def draw_elem_count(key, part):
    first_key = jax.random.fold_in(key, 11)
    second_key = jax.random.fold_in(key, 12)
    third_key = jax.random.fold_in(key, 13)
    draw_one = jax.random.randint(first_key, (BLOCKS,), 1, E_CAP + 1)
    draw_two = jax.random.randint(second_key, (BLOCKS,), 1, E_CAP + 1)
    counts = jnp.minimum(draw_one, draw_two)
    busiest = jax.random.randint(third_key, (), 0, BLOCKS)
    return jnp.where(jnp.arange(BLOCKS) == busiest, E_CAP, counts).astype(jnp.int32)


def draw_elem_matrix(key, part):
    normals = jnp.clip(jax.random.normal(jax.random.fold_in(key, 21), (ELEM_NODES, ELEM_NODES), jnp.float32), -4.0, 4.0)
    matrix = (normals + normals.T) / jnp.sqrt(2.0 * ELEM_NODES)
    return matrix.astype(jnp.bfloat16)


def touch_ends(result, rng, least, top_value):
    longest = result.shape.index(max(result.shape))
    spots = []
    for shift in (0, 1):
        where = [jax.random.randint(jax.random.fold_in(rng, axis), (), 0, length) for axis, length in enumerate(result.shape)]
        where[longest] = (where[longest] + shift) % result.shape[longest]
        spots.append(tuple(where))
    return result.at[spots[0]].set(least).at[spots[1]].set(top_value)


def levels(stream_key, extent, cuts, smallest, high):
    def one(dim, parts):
        heights = jax.random.uniform(jax.random.fold_in(jax.random.fold_in(stream_key, 6), dim), (parts,), jnp.float32, smallest / len(cuts), high / len(cuts))
        return jnp.repeat(jnp.exp(heights), extent[dim] // parts).reshape((-1,) + (1,) * (len(extent) - dim - 1))

    loudness = one(*cuts[0])
    for cut in cuts[1:]:
        loudness = loudness * one(*cut)
    return loudness


def centred(rng, extent, width, most, pieces=(), kind=jnp.bfloat16):
    drawn = jax.random.normal(rng, extent, jnp.float32) * width
    if len(pieces) > 0:
        drawn = levels(rng, extent, pieces, -0.22, 0.18) * drawn
    return jnp.clip(drawn, min=-most, max=most).astype(kind)


def setup_inputs(seed: int = 0) -> dict:
    seeds = jax.random.split(jax.random.key(seed), 9)
    orbitals = centred(seeds[0], (NODES, 2, BANDS), 1.0, 6.0, ((0, 192), (2, 4)))
    elem_count = draw_elem_count(jax.random.fold_in(seeds[8], 71), 0)
    connectivity = touch_ends(jax.random.randint(seeds[2], (BLOCKS, E_CAP, ELEM_NODES), 0, NODE_DEV + 2 * FACE), jax.random.fold_in(seeds[2], 1), 0, (NODE_DEV + 2 * FACE) - 1).astype(jnp.int32)
    elem_coef = jnp.clip(jnp.exp(math.log(2.0) - 1.3862944 * jax.random.uniform(seeds[3], (BLOCKS, E_CAP), jnp.float32) ** levels(seeds[3], (BLOCKS, E_CAP), ((0, 192),), -0.2, 0.2)), 0.5, 2.0)
    elem_matrix = draw_elem_matrix(jax.random.fold_in(seeds[8], 71), 0)
    potential = jnp.clip(jax.random.uniform(seeds[5], (NODES,), jnp.float32, -1.0, 1.0) * levels(seeds[5], (NODES,), ((0, 192),), -0.4, 0.0), -1.0, 1.0)
    absorber = jnp.clip(jnp.exp(math.log(1.0) - 2.9957323 * jax.random.uniform(seeds[6], (NODES,), jnp.float32) ** levels(seeds[6], (NODES,), ((0, 192),), -0.2, 0.2)), 0.05, 1.0)
    rotation = centred(seeds[7], (BANDS, 2, PANEL), (2 * BANDS) ** -0.5, 0.109375)
    return dict(orbitals=orbitals, elem_count=elem_count, connectivity=connectivity, elem_coef=elem_coef, elem_matrix=elem_matrix, potential=potential, absorber=absorber, rotation=rotation)


FILTER_CENTER = 1.0
FILTER_HALF = 4.0

def assemble(field, elem_count, connectivity, elem_coef, elem_matrix):
    width_all = field.shape[1] * field.shape[2]
    flat_field = field.reshape(NODES, width_all)
    padded = jnp.pad(flat_field, ((FACE, FACE), (0, 0)))

    def one_block(inputs):
        block_id, live_count, node_lists, coefs = inputs
        extended = lax.dynamic_slice_in_dim(padded, (block_id * NODE_DEV).astype(jnp.int32), NODE_DEV + 2 * FACE, 0)
        totals = jnp.zeros((NODE_DEV + 2 * FACE, width_all), jnp.float32)
        for element in range(E_CAP):
            node_ids = node_lists[element]
            factor = coefs[element] * (element < live_count).astype(jnp.float32)
            product = jnp.dot(elem_matrix, extended[node_ids], preferred_element_type=jnp.float32)
            totals = totals.at[node_ids].add(product * factor)
        return totals
    blocks = lax.map(one_block, (jnp.arange(BLOCKS, dtype=jnp.int32), elem_count, connectivity, elem_coef))
    owned = blocks[:, FACE:FACE + NODE_DEV]
    owned = owned.at[1:, :FACE].add(blocks[:-1, FACE + NODE_DEV:])
    owned = owned.at[:-1, NODE_DEV - FACE:].add(blocks[1:, :FACE])
    return owned.reshape(field.shape)

def hamiltonian(field, elem_count, connectivity, elem_coef, elem_matrix, potential, absorber):
    summed = assemble(field, elem_count, connectivity, elem_coef, elem_matrix)
    vector = field.astype(jnp.float32)
    pot_col = potential[:, None]
    cap_col = absorber[:, None]
    ham_re = summed[:, 0] + pot_col * vector[:, 0] + cap_col * vector[:, 1]
    ham_im = summed[:, 1] + pot_col * vector[:, 1] - cap_col * vector[:, 0]
    return (ham_re, ham_im, vector)

def reference(orbitals, elem_count, connectivity, elem_coef, elem_matrix, potential, absorber, rotation):
    ham_re, ham_im, vector = hamiltonian(orbitals, elem_count, connectivity, elem_coef, elem_matrix, potential, absorber)
    first = jnp.stack([(ham_re - FILTER_CENTER * vector[:, 0]) / FILTER_HALF, (ham_im - FILTER_CENTER * vector[:, 1]) / FILTER_HALF], axis=1).astype(jnp.bfloat16)
    ham_re, ham_im, inner = hamiltonian(first, elem_count, connectivity, elem_coef, elem_matrix, potential, absorber)
    anchor = orbitals.astype(jnp.float32)
    filtered = jnp.stack([2.0 * (ham_re - FILTER_CENTER * inner[:, 0]) / FILTER_HALF - anchor[:, 0], 2.0 * (ham_im - FILTER_CENTER * inner[:, 1]) / FILTER_HALF - anchor[:, 1]], axis=1).astype(jnp.bfloat16)
    flat_bands = filtered.reshape(NODES, 2 * BANDS)
    rot_re = rotation[:, 0]
    rot_im = rotation[:, 1]
    block_matrix = jnp.concatenate([jnp.concatenate([rot_re, rot_im], axis=1), jnp.concatenate([-rot_im, rot_re], axis=1)], axis=0)
    rotated = jnp.dot(flat_bands, block_matrix, preferred_element_type=jnp.float32).astype(jnp.bfloat16).reshape(NODES, 2, PANEL)
    flat_panel = rotated.reshape(NODES, 2 * PANEL)
    products = lax.dot_general(flat_bands, flat_panel, (((0,), (0,)), ((), ())), preferred_element_type=jnp.float32)
    products = products.reshape(2, BANDS, 2, PANEL)
    over_re = products[0, :, 0] - products[1, :, 1]
    over_im = products[0, :, 1] + products[1, :, 0]
    intersection = jnp.stack([over_re, over_im], axis=1) * (1.0 / math.sqrt(NODES))
    return (filtered, rotated, intersection)
```

```python
import functools

import jax
import jax.numpy as jnp
from jax import lax
from jax.experimental import pallas as pl
from jax.experimental.pallas import tpu as pltpu
from jax.sharding import PartitionSpec as P

MESH = pl.DeviceIdType.MESH
FILTER_CENTER = 1.0
FILTER_HALF = 4.0

N = 128
C = 3
NX, NY, NZ = 4, 4, 12
BLOCKS = NX * NY * NZ
JP = 384
PREV, OWN, NEXT = 0, 1, 2


def body(
    orb, pack, mat, diag, rot, filt_out, rot_out, inter_out,
    pk, sacc, s2, vext, fext, qv, yall, racc, rr, wacc, wsend, recvx, xs, xsb,
    recvy, ys, ysb, recvz, ag,
    loc_sem, out_sem, pk_ss, pk_rs, h_ss, h_rs, y_ss, y_rs, x_ss, x_rs, x2_ss, x2_rs, z_ss, z_rs, az_ss, az_rs,
    ay_ss, ay_rs, ax_ss, ax_rs,
):
    b = lax.axis_index("elem")
    k = lax.axis_index("band")
    xi = lax.rem(b, NX)
    yi = lax.rem(lax.div(b, NX), NY)
    zi = lax.div(b, NX * NY)
    k1 = k + 1 - 2 * lax.rem(k, 2)
    k2 = lax.rem(k + 2, 4)
    k3 = 3 - k
    has_left = b > 0
    has_right = b < BLOCKS - 1

    def x_peer(d):
        return b - xi + lax.rem(xi + d, NX)

    def y_peer(d):
        return b + (lax.rem(yi + d, NY) - yi) * NX

    def z_peer(d):
        return b + (lax.rem(zi + d, NZ) - zi) * (NX * NY)

    barrier = pltpu.get_barrier_semaphore()

    def greet(e, kk):
        pl.semaphore_signal(barrier, inc=1, device_id=(e, kk), device_id_type=MESH)

    @pl.when(has_left)
    def _():
        greet(b - 1, k)

    @pl.when(has_right)
    def _():
        greet(b + 1, k)

    greet(b, k1)
    greet(b, k2)
    for d in range(1, NX):
        greet(x_peer(d), k)
    for d in range(1, NY):
        greet(y_peer(d), k)
    for d in range(1, NZ):
        greet(z_peer(d), k)

    own_rows = pl.ds(2 * N, N)
    load_orb = pltpu.make_async_copy(orb, vext.at[:, own_rows, :], loc_sem.at[0])
    load_orb.start()
    load_pk = pltpu.make_async_copy(pack, pk.at[OWN], loc_sem.at[1])
    load_pk.start()
    load_q = pltpu.make_async_copy(rot, qv, loc_sem.at[2])
    load_q.start()

    @pl.when(b < 2)
    def _():
        zeros = jnp.zeros((C, N, 2 * N), jnp.bfloat16)
        vext[:, 0:N, :] = zeros
        fext[:, 0:N, :] = zeros

    @pl.when(b < 1)
    def _():
        zeros = jnp.zeros((C, N, 2 * N), jnp.bfloat16)
        vext[:, N : 2 * N, :] = zeros
        fext[:, N : 2 * N, :] = zeros
        pk[PREV] = jnp.zeros(pk.shape[1:], jnp.float32)

    @pl.when(b > BLOCKS - 3)
    def _():
        zeros = jnp.zeros((C, N, 2 * N), jnp.bfloat16)
        vext[:, 4 * N : 5 * N, :] = zeros
        fext[:, 4 * N : 5 * N, :] = zeros

    @pl.when(b > BLOCKS - 2)
    def _():
        zeros = jnp.zeros((C, N, 2 * N), jnp.bfloat16)
        vext[:, 3 * N : 4 * N, :] = zeros
        fext[:, 3 * N : 4 * N, :] = zeros
        pk[NEXT] = jnp.zeros(pk.shape[1:], jnp.float32)

    sacc[...] = jnp.zeros(sacc.shape, jnp.float32)

    def add_strip(which):
        first_row = (2 - which) * N

        def one(e, carry):
            ids = pk[which, pl.ds(e, 1), :]
            factor = pk[which, pl.ds(e + 4, 1), :]
            nodes = lax.broadcasted_iota(jnp.int32, (JP, JP), 0).astype(jnp.float32)
            picks = jnp.where(nodes == ids, 1.0, 0.0).astype(jnp.bfloat16)
            mine = picks[first_row : first_row + N]
            part = jnp.dot(mine, mat[...], preferred_element_type=jnp.float32) * factor
            high = part.astype(jnp.bfloat16)
            low = (part - high.astype(jnp.float32)).astype(jnp.bfloat16)
            both = jnp.concatenate([high, low], axis=0)
            got = lax.dot_general(both, picks, (((1,), (1,)), ((), ())), preferred_element_type=jnp.float32)
            cols = slice(which * N, which * N + JP)
            sacc[:, cols] = sacc[:, cols] + got[:N] + got[N:]
            return carry

        lax.fori_loop(0, 4, one, 0)

    load_pk.wait()
    add_strip(OWN)
    load_orb.wait()
    pl.semaphore_wait(barrier, 2 + NX - 1 + NY - 1 + NZ - 1 + has_left.astype(jnp.int32) + has_right.astype(jnp.int32))

    def remote(src, dst, ss, rs, e, kk):
        return pltpu.make_async_remote_copy(
            src_ref=src, dst_ref=dst, send_sem=ss, recv_sem=rs, device_id=(e, kk), device_id_type=MESH
        )

    def hop(buf, rnd, c, col):
        src_slot, dst_slot, step = ((2, 1, 1), (2, 3, -1), (1, 0, 1), (3, 4, -1))[col]
        return remote(
            buf.at[c, pl.ds(src_slot * N, N), :],
            buf.at[c, pl.ds(dst_slot * N, N), :],
            h_ss.at[rnd, c, col],
            h_rs.at[rnd, c, col],
            b + step,
            k,
        )

    pk_right = remote(pk.at[OWN], pk.at[PREV], pk_ss.at[0], pk_rs.at[0], b + 1, k)
    pk_left = remote(pk.at[OWN], pk.at[NEXT], pk_ss.at[1], pk_rs.at[1], b - 1, k)

    @pl.when(has_right)
    def _():
        pk_right.start()

    @pl.when(has_left)
    def _():
        pk_left.start()

    def send_own(buf, rnd, c):
        @pl.when(has_right)
        def _():
            hop(buf, rnd, c, 0).start()

        @pl.when(has_left)
        def _():
            hop(buf, rnd, c, 1).start()

    def relay(buf, rnd, c):
        @pl.when(has_left)
        def _():
            hop(buf, rnd, c, 0).wait_recv()

        @pl.when(has_left & has_right)
        def _():
            hop(buf, rnd, c, 2).start()

        @pl.when(has_right)
        def _():
            hop(buf, rnd, c, 1).wait_recv()

        @pl.when(has_left & has_right)
        def _():
            hop(buf, rnd, c, 3).start()

    def arrived(buf, rnd, c):
        @pl.when(b > 1)
        def _():
            hop(buf, rnd, c, 2).wait_recv()

        @pl.when(b < BLOCKS - 2)
        def _():
            hop(buf, rnd, c, 3).wait_recv()

    for c in range(C):
        send_own(vext, 0, c)

    @pl.when(has_left)
    def _():
        pk_right.wait_recv()

    relay(vext, 0, 0)
    add_strip(PREV)

    @pl.when(has_right)
    def _():
        pk_left.wait_recv()

    relay(vext, 0, 1)
    add_strip(NEXT)
    relay(vext, 0, 2)

    high = sacc[...].astype(jnp.bfloat16)
    s2[0:N, :] = high
    s2[N : 2 * N, :] = (sacc[...] - high.astype(jnp.float32)).astype(jnp.bfloat16)

    def apply(buf, c):
        both = jnp.dot(s2[...], buf[c], preferred_element_type=jnp.float32)
        k_v = both[:N] + both[N:]
        own = buf[c, 2 * N : 3 * N, :].astype(jnp.float32)
        v_re, v_im = own[:, :N], own[:, N:]
        pot, cap = diag[:, 0:1], diag[:, 1:2]
        ham_re = k_v[:, :N] + pot * v_re + cap * v_im
        ham_im = k_v[:, N:] + pot * v_im - cap * v_re
        return (ham_re - FILTER_CENTER * v_re), (ham_im - FILTER_CENTER * v_im)

    for c in range(C):
        arrived(vext, 0, c)
        re, im = apply(vext, c)
        fext[c, 2 * N : 3 * N, 0:N] = (re / FILTER_HALF).astype(jnp.bfloat16)
        fext[c, 2 * N : 3 * N, N : 2 * N] = (im / FILTER_HALF).astype(jnp.bfloat16)
        send_own(fext, 1, c)
    for c in range(C):
        relay(fext, 1, c)

    def y_copy(c, col):
        src, dst, kk = ((0, 1, k1), (0, 2, k2), (2, 3, k1))[col]
        return remote(yall.at[src, c], yall.at[dst, c], y_ss.at[c, col], y_rs.at[c, col], b, kk)

    def turned(slot, c):
        y = yall[slot, c]
        y_re, y_im = y[:, :N], y[:, N:]
        return jnp.concatenate(
            [jnp.concatenate([y_re, -y_im], axis=1), jnp.concatenate([y_im, y_re], axis=1)], axis=0
        )

    racc[...] = jnp.zeros(racc.shape, jnp.float32)

    def add_rotated(slot, c, kk):
        racc[...] = racc[...] + jnp.dot(
            turned(slot, c), qv[kk * C + c], preferred_element_type=jnp.float32
        )

    for c in range(C):
        arrived(fext, 1, c)
        re, im = apply(fext, c)
        anchor = vext[c, 2 * N : 3 * N, :].astype(jnp.float32)
        yall[0, c, :, 0:N] = (2.0 * re / FILTER_HALF - anchor[:, :N]).astype(jnp.bfloat16)
        yall[0, c, :, N : 2 * N] = (2.0 * im / FILTER_HALF - anchor[:, N:]).astype(jnp.bfloat16)
        y_copy(c, 1).start()
        y_copy(c, 0).start()
    filt_copy = pltpu.make_async_copy(yall.at[0], filt_out, out_sem.at[0])
    filt_copy.start()
    load_q.wait()
    for c in range(C):
        add_rotated(0, c, k)
    for c in range(C):
        y_copy(c, 0).wait_recv()
        add_rotated(1, c, k1)
    for c in range(C):
        y_copy(c, 1).wait_recv()
        y_copy(c, 2).start()
        add_rotated(2, c, k2)
    for c in range(C):
        y_copy(c, 2).wait_recv()
        add_rotated(3, c, k3)

    for i in range(NX):
        rr[i] = racc[:, i * N : (i + 1) * N].astype(jnp.bfloat16)
    rot_copy = pltpu.make_async_copy(rr.at[k], rot_out, out_sem.at[1])
    rot_copy.start()

    for c in range(C):
        y = yall[0, c]
        y_re, y_im = y[:, :N], y[:, N:]
        left = jnp.concatenate(
            [jnp.concatenate([y_re, y_im], axis=1), jnp.concatenate([-y_im, y_re], axis=1)], axis=0
        )
        right = jnp.concatenate([rr[i] for i in range(NX)], axis=1)
        got = lax.dot_general(left, right, (((0,), (0,)), ((), ())), preferred_element_type=jnp.float32)
        for i in range(NX):
            piece = got[:, i * N : (i + 1) * N]
            wacc[i, c * 256 : (c + 1) * 256, :] = piece
            wsend[i, c * 256 : (c + 1) * 256, :] = piece.astype(jnp.bfloat16)

    def x_copy(d):
        return remote(wsend.at[lax.rem(xi + d, NX)], recvx.at[d - 1], x_ss.at[d - 1], x_rs.at[d - 1], x_peer(d), k)

    for d in (2, 1, 3):
        x_copy(d).start()
    for d in (1, 3, 2):
        x_copy(d).wait_recv()
    for j in range(NY):
        rows = slice(j * 192, (j + 1) * 192)
        total = wacc[xi, rows, :]
        for d in range(NX - 1):
            total = total + recvx[d, rows, :].astype(jnp.float32)
        xs[j] = total
        xsb[j] = total.astype(jnp.bfloat16)

    def y2_copy(d):
        return remote(xsb.at[lax.rem(yi + d, NY)], recvy.at[d - 1], x2_ss.at[d - 1], x2_rs.at[d - 1], y_peer(d), k)

    for d in range(1, NY):
        y2_copy(d).start()
    for d in range(1, NY):
        y2_copy(d).wait_recv()
    total = xs[yi]
    for d in range(NY - 1):
        total = total + recvy[d].astype(jnp.float32)
    ys[...] = total.reshape(NZ, 16, N)
    ysb[...] = total.astype(jnp.bfloat16).reshape(NZ, 16, N)

    def z_copy(d):
        return remote(ysb.at[lax.rem(zi + d, NZ)], recvz.at[d - 1], z_ss.at[d - 1], z_rs.at[d - 1], z_peer(d), k)

    far_first = (6, 5, 7, 4, 8, 3, 9, 2, 10, 1, 11)
    for d in far_first:
        z_copy(d).start()
    for d in range(1, NZ):
        z_copy(d).wait_recv()
    total = ys[zi]
    for d in range(NZ - 1):
        total = total + recvz[d].astype(jnp.float32)
    inverse_root = 1.0 / jnp.sqrt(jnp.float32(N * BLOCKS))
    ag[xi, yi, zi] = (total * inverse_root).astype(jnp.bfloat16)

    def az_copy(d):
        piece = ag.at[xi, yi, zi]
        return remote(piece, piece, az_ss.at[d - 1], az_rs.at[d - 1], z_peer(d), k)

    for d in far_first:
        az_copy(d).start()
    for d in range(1, NZ):
        az_copy(d).wait_recv()

    def ay_copy(d):
        piece = ag.at[xi, yi]
        return remote(piece, piece, ay_ss.at[d - 1], ay_rs.at[d - 1], y_peer(d), k)

    for d in range(1, NY):
        ay_copy(d).start()
    for d in range(1, NY):
        ay_copy(d).wait_recv()

    def ax_copy(d):
        piece = ag.at[xi]
        return remote(piece, piece, ax_ss.at[d - 1], ax_rs.at[d - 1], x_peer(d), k)

    for d in (2, 1, 3):
        ax_copy(d).start()
    for d in (1, 3, 2):
        ax_copy(d).wait_recv()
    inter_copy = pltpu.make_async_copy(ag, inter_out, out_sem.at[2])
    inter_copy.start()

    @pl.when(has_right)
    def _():
        pk_right.wait_send()

    @pl.when(has_left)
    def _():
        pk_left.wait_send()

    for rnd, buf in ((0, vext), (1, fext)):
        for c in range(C):
            @pl.when(has_right)
            def _():
                hop(buf, rnd, c, 0).wait_send()

            @pl.when(has_left)
            def _():
                hop(buf, rnd, c, 1).wait_send()

            @pl.when(has_left & has_right)
            def _():
                hop(buf, rnd, c, 2).wait_send()
                hop(buf, rnd, c, 3).wait_send()

    for c in range(C):
        for col in range(3):
            y_copy(c, col).wait_send()
    for d in range(1, NX):
        x_copy(d).wait_send()
        ax_copy(d).wait_send()
    for d in range(1, NY):
        y2_copy(d).wait_send()
        ay_copy(d).wait_send()
    for d in range(1, NZ):
        z_copy(d).wait_send()
        az_copy(d).wait_send()
    filt_copy.wait()
    rot_copy.wait()
    inter_copy.wait()


def on_device(orbitals, elem_count, connectivity, elem_coef, elem_matrix, potential, absorber, rotation):
    f32, bf16 = jnp.float32, jnp.bfloat16
    nodes = elem_matrix.shape[0]
    orb = orbitals.reshape(N, 2, C, N).transpose(2, 0, 1, 3).reshape(C, N, 2 * N)
    rot = rotation.reshape(4 * C, N, 2, 4 * N).transpose(0, 2, 1, 3).reshape(4 * C, 2 * N, 4 * N)
    mat = jnp.pad(elem_matrix, ((0, JP - nodes), (0, JP - nodes)))
    ids = jnp.pad(connectivity[0].astype(f32), ((0, 0), (0, JP - nodes)), constant_values=-1.0)
    live = jnp.where(jnp.arange(4) < elem_count[0], elem_coef[0], 0.0)
    pack = jnp.concatenate([ids, jnp.broadcast_to(live[:, None], (4, JP))], axis=0)
    diag = jnp.stack([potential, absorber], axis=1)
    hbm = pl.BlockSpec(memory_space=pl.ANY)
    vmem = pl.BlockSpec(memory_space=pltpu.VMEM)
    dma = pltpu.SemaphoreType.DMA
    filt, rotated, inter = pl.pallas_call(
        body,
        out_shape=(
            jax.ShapeDtypeStruct((C, N, 2 * N), bf16),
            jax.ShapeDtypeStruct((2 * N, N), bf16),
            jax.ShapeDtypeStruct((NX, NY, NZ, 16, N), bf16),
        ),
        in_specs=[hbm, hbm, vmem, vmem, hbm],
        out_specs=(hbm, hbm, hbm),
        scratch_shapes=[
            pltpu.VMEM((3, 8, JP), f32),
            pltpu.VMEM((N, 5 * N), f32),
            pltpu.VMEM((2 * N, 5 * N), bf16),
            pltpu.VMEM((C, 5 * N, 2 * N), bf16),
            pltpu.VMEM((C, 5 * N, 2 * N), bf16),
            pltpu.VMEM((4 * C, 2 * N, 4 * N), bf16),
            pltpu.VMEM((4, C, N, 2 * N), bf16),
            pltpu.VMEM((2 * N, 4 * N), f32),
            pltpu.VMEM((4, 2 * N, N), bf16),
            pltpu.VMEM((NX, 6 * N, N), f32),
            pltpu.VMEM((NX, 6 * N, N), bf16),
            pltpu.VMEM((NX - 1, 6 * N, N), bf16),
            pltpu.VMEM((NY, 192, N), f32),
            pltpu.VMEM((NY, 192, N), bf16),
            pltpu.VMEM((NY - 1, 192, N), bf16),
            pltpu.VMEM((NZ, 16, N), f32),
            pltpu.VMEM((NZ, 16, N), bf16),
            pltpu.VMEM((NZ - 1, 16, N), bf16),
            pltpu.VMEM((NX, NY, NZ, 16, N), bf16),
            dma((3,)), dma((3,)),
            dma((2,)), dma((2,)),
            dma((2, C, 4)), dma((2, C, 4)),
            dma((C, 3)), dma((C, 3)),
            dma((NX - 1,)), dma((NX - 1,)),
            dma((NY - 1,)), dma((NY - 1,)),
            dma((NZ - 1,)), dma((NZ - 1,)),
            dma((NZ - 1,)), dma((NZ - 1,)),
            dma((NY - 1,)), dma((NY - 1,)),
            dma((NX - 1,)), dma((NX - 1,)),
        ],
        compiler_params=pltpu.CompilerParams(collective_id=0, has_side_effects=True, vmem_limit_bytes=48 << 20),
        name="filter_panel",
    )(orb, pack, mat, diag, rot)
    filtered = filt.reshape(C, N, 2, N).transpose(1, 2, 0, 3).reshape(N, 2, C * N)
    rotated = rotated.reshape(2, N, N).transpose(1, 0, 2)
    inter = inter.reshape(NX, C, 2, N, N).transpose(1, 3, 2, 0, 4).reshape(C * N, 2, NX * N)
    return (filtered, rotated, inter.astype(f32))


def solution(mesh):
    placed = (
        P("elem", None, "band"),
        P("elem"),
        P("elem", None, None),
        P("elem", None),
        P(),
        P("elem"),
        P("elem"),
        P(),
    )
    return jax.shard_map(
        on_device,
        mesh=mesh,
        in_specs=placed,
        out_specs=(P("elem", None, "band"), P("elem", None, "band"), P("band", None, None)),
        check_vma=False,
    )
```

```python
import functools

import jax
import jax.numpy as jnp
from jax import lax
from jax.experimental import pallas as pl
from jax.experimental.pallas import tpu as pltpu
from jax.sharding import PartitionSpec as P

MESH = pl.DeviceIdType.MESH
FILTER_CENTER = 1.0
FILTER_HALF = 4.0

N = 128
C = 3
NX, NY, NZ = 4, 4, 12
BLOCKS = NX * NY * NZ
JP = 384
PREV, OWN, NEXT = 0, 1, 2


def body(
    orb, ids_in, coef_in, count_in, mat_in, pot_in, cap_in, rot, filt_out, rot_out, inter_out,
    pk, mat, diag, gall, gmine, both, sacc, s2, orb_raw, vext, fext, q_raw, qv, yall, left_t, racc, rr, wacc, wsend, recvx, xs, xsb,
    recvy, ys, ysb, recvz, ag,
    orb_sem, q_sem, filt_sem, rot_sem, inter_sem, pk_ss, pk_rs, h_ss, h_rs, y_ss, y_rs, x_ss, x_rs,
    x2_ss, x2_rs, z_ss, z_rs, az_ss, az_rs, ay_ss, ay_rs, ax_ss, ax_rs,
):
    f32, bf16 = jnp.float32, jnp.bfloat16
    b = lax.axis_index("elem")
    k = lax.axis_index("band")
    xi = lax.rem(b, NX)
    yi = lax.rem(lax.div(b, NX), NY)
    zi = lax.div(b, NX * NY)
    k1 = k + 1 - 2 * lax.rem(k, 2)
    k2 = lax.rem(k + 2, 4)
    k3 = 3 - k
    has_left = b > 0
    has_right = b < BLOCKS - 1

    def x_peer(d):
        return b - xi + lax.rem(xi + d, NX)

    def y_peer(d):
        return b + (lax.rem(yi + d, NY) - yi) * NX

    def z_peer(d):
        return b + (lax.rem(zi + d, NZ) - zi) * (NX * NY)

    barrier = pltpu.get_barrier_semaphore()

    def greet(e, kk):
        pl.semaphore_signal(barrier, inc=1, device_id=(e, kk), device_id_type=MESH)

    for d in range(1, NZ):
        greet(z_peer(d), k)

    @pl.when(has_left)
    def _():
        greet(b - 1, k)

    @pl.when(has_right)
    def _():
        greet(b + 1, k)

    greet(b, k2)
    for d in range(1, NY):
        greet(y_peer(d), k)
    for d in range(1, NX):
        greet(x_peer(d), k)
    greet(b, k1)

    load_orb = pltpu.make_async_copy(orb, orb_raw, orb_sem.at[0])
    load_orb.start()
    load_q = pltpu.make_async_copy(rot, q_raw, q_sem.at[0])
    load_q.start()

    def clear(slot):
        zeros = jnp.zeros((C, N, 2 * N), bf16)
        vext[:, slot * N : (slot + 1) * N, :] = zeros
        fext[:, slot * N : (slot + 1) * N, :] = zeros

    @pl.when(b < 2)
    def _():
        clear(0)

    @pl.when(b < 1)
    def _():
        clear(1)
        pk[PREV] = jnp.zeros(pk.shape[1:], f32)

    @pl.when(b > BLOCKS - 3)
    def _():
        clear(4)

    @pl.when(b > BLOCKS - 2)
    def _():
        clear(3)
        pk[NEXT] = jnp.zeros(pk.shape[1:], f32)

    nodes = mat_in.shape[0]
    pk[OWN] = jnp.full(pk.shape[1:], -1.0, f32)
    pk[OWN, 0:4, 0:nodes] = ids_in[0].astype(f32)
    live = jnp.where(lax.broadcasted_iota(jnp.int32, (1, 4), 1) < count_in[...], coef_in[...], 0.0)
    for e in range(4):
        pk[OWN, 4 + e : 5 + e, :] = jnp.broadcast_to(live[:, e : e + 1], (1, JP))

    load_orb.wait()
    planes = jnp.swapaxes(orb_raw[...], 0, 1)
    for c in range(C):
        for p in range(2):
            vext[c, 2 * N : 3 * N, p * N : (p + 1) * N] = planes[p, :, c * N : (c + 1) * N]
    pl.semaphore_wait(barrier, 2 + NX - 1 + NY - 1 + NZ - 1 + has_left.astype(jnp.int32) + has_right.astype(jnp.int32))

    def remote(src, dst, ss, rs, e, kk):
        return pltpu.make_async_remote_copy(
            src_ref=src, dst_ref=dst, send_sem=ss, recv_sem=rs, device_id=(e, kk), device_id_type=MESH
        )

    def hop(buf, rnd, c, col):
        src_slot, dst_slot, step = ((2, 1, 1), (2, 3, -1), (1, 0, 1), (3, 4, -1))[col]
        return remote(
            buf.at[c, pl.ds(src_slot * N, N), :],
            buf.at[c, pl.ds(dst_slot * N, N), :],
            h_ss.at[rnd, c, col],
            h_rs.at[rnd, c, col],
            b + step,
            k,
        )

    pk_right = remote(pk.at[OWN], pk.at[PREV], pk_ss.at[0], pk_rs.at[0], b + 1, k)
    pk_left = remote(pk.at[OWN], pk.at[NEXT], pk_ss.at[1], pk_rs.at[1], b - 1, k)

    @pl.when(has_right)
    def _():
        pk_right.start()

    @pl.when(has_left)
    def _():
        pk_left.start()

    def send_own(buf, rnd, c):
        @pl.when(has_right)
        def _():
            hop(buf, rnd, c, 0).start()

        @pl.when(has_left)
        def _():
            hop(buf, rnd, c, 1).start()

    def from_left(buf, rnd, c):
        @pl.when(has_left)
        def _():
            hop(buf, rnd, c, 0).wait_recv()

        @pl.when(has_left & has_right)
        def _():
            hop(buf, rnd, c, 2).start()

    def from_right(buf, rnd, c):
        @pl.when(has_right)
        def _():
            hop(buf, rnd, c, 1).wait_recv()

        @pl.when(has_left & has_right)
        def _():
            hop(buf, rnd, c, 3).start()

    def relay(buf, rnd, near, even, far):
        @pl.when(xi == 0)
        def _():
            for c in near:
                from_right(buf, rnd, c)
            for c in far:
                from_left(buf, rnd, c)

        @pl.when(xi == NX - 1)
        def _():
            for c in near:
                from_left(buf, rnd, c)
            for c in far:
                from_right(buf, rnd, c)

        @pl.when((xi > 0) & (xi < NX - 1))
        def _():
            for c in even:
                from_left(buf, rnd, c)
                from_right(buf, rnd, c)

    def arrived(buf, rnd, c):
        @pl.when(b > 1)
        def _():
            hop(buf, rnd, c, 2).wait_recv()

        @pl.when(b < BLOCKS - 2)
        def _():
            hop(buf, rnd, c, 3).wait_recv()

    for c in range(C):
        send_own(vext, 0, c)

    mat[...] = jnp.zeros(mat.shape, bf16)
    mat[0:nodes, 0:nodes] = mat_in[...]
    diag[0] = jnp.transpose(jnp.broadcast_to(pot_in[...], (N, N)))
    diag[1] = jnp.transpose(jnp.broadcast_to(cap_in[...], (N, N)))
    sacc[...] = jnp.zeros(sacc.shape, f32)

    def add_strip(which):
        rows = pk[which]
        columns = jnp.transpose(rows)
        lanes = lax.broadcasted_iota(jnp.int32, (JP, JP), 1).astype(f32)
        mine = (lax.broadcasted_iota(jnp.int32, (N, JP), 0) + (2 - which) * N).astype(f32)
        for e in range(4):
            gall[e * JP : (e + 1) * JP, :] = jnp.where(lanes == columns[:, e : e + 1], 1.0, 0.0).astype(bf16)
            gmine[e * N : (e + 1) * N, :] = jnp.where(mine == rows[e : e + 1, :], 1.0, 0.0).astype(bf16)
        part = jnp.dot(gmine[...], mat[...], preferred_element_type=f32)
        for e in range(4):
            term = part[e * N : (e + 1) * N] * rows[4 + e : 5 + e, :]
            high = term.astype(bf16)
            both[0:N, e * JP : (e + 1) * JP] = high
            both[N : 2 * N, e * JP : (e + 1) * JP] = (term - high.astype(f32)).astype(bf16)
        got = jnp.dot(both[...], gall[...], preferred_element_type=f32)
        cols = pl.ds(pl.multiple_of(which * N, N), JP)
        sacc[:, cols] = sacc[:, cols] + got[:N] + got[N:]

    def pack_from_left():
        @pl.when(has_left)
        def _():
            pk_right.wait_recv()

    def pack_from_right():
        @pl.when(has_right)
        def _():
            pk_left.wait_recv()

    add_strip(OWN)
    relay(vext, 0, (0, 1), (0,), ())
    right_first = xi == 0

    @pl.when(right_first)
    def _():
        pack_from_right()

    @pl.when(xi > 0)
    def _():
        pack_from_left()

    step = right_first.astype(jnp.int32)
    add_strip(2 * step)
    relay(vext, 0, (2,), (1,), ())

    @pl.when(right_first)
    def _():
        pack_from_left()

    @pl.when(xi > 0)
    def _():
        pack_from_right()

    add_strip(2 - 2 * step)
    relay(vext, 0, (), (2,), (0, 1, 2))

    high = sacc[...].astype(bf16)
    s2[0:N, :] = high
    s2[N : 2 * N, :] = (sacc[...] - high.astype(f32)).astype(bf16)

    def apply(buf, c):
        two = jnp.dot(s2[...], buf[c], preferred_element_type=f32)
        k_v = two[:N] + two[N:]
        own = buf[c, 2 * N : 3 * N, :].astype(f32)
        v_re, v_im = own[:, :N], own[:, N:]
        ham_re = k_v[:, :N] + diag[0] * v_re + diag[1] * v_im
        ham_im = k_v[:, N:] + diag[0] * v_im - diag[1] * v_re
        return (ham_re - FILTER_CENTER * v_re), (ham_im - FILTER_CENTER * v_im)

    def split_rotation(first, last):
        def one(i, carry):
            planes = jnp.swapaxes(q_raw[pl.ds(pl.multiple_of(i * N, N), N)], 0, 1)
            qv[i, 0:N, :] = planes[0]
            qv[i, N : 2 * N, :] = planes[1]
            return carry

        lax.fori_loop(first, last, one, 0)

    load_q.wait()
    split_rotation(0, 2 * C)
    for c in range(C):
        arrived(vext, 0, c)
        re, im = apply(vext, c)
        fext[c, 2 * N : 3 * N, 0:N] = (re / FILTER_HALF).astype(bf16)
        fext[c, 2 * N : 3 * N, N : 2 * N] = (im / FILTER_HALF).astype(bf16)
        send_own(fext, 1, c)
    split_rotation(2 * C, 4 * C)
    relay(fext, 1, (0, 1, 2), (0, 1, 2), (0, 1, 2))

    def y_copy(c, col):
        src, dst, kk = ((0, 1, k1), (0, 2, k2), (2, 3, k1))[col]
        return remote(yall.at[src, c], yall.at[dst, c], y_ss.at[c, col], y_rs.at[c, col], b, kk)

    def add_rotated(slot, c, kk):
        y = yall[slot, c]
        y_re, y_im = y[:, :N], y[:, N:]
        turned = jnp.concatenate(
            [jnp.concatenate([y_re, -y_im], axis=1), jnp.concatenate([y_im, y_re], axis=1)], axis=0
        )
        racc[...] = racc[...] + jnp.dot(turned, qv[kk * C + c], preferred_element_type=f32)

    racc[...] = jnp.zeros(racc.shape, f32)
    filt_copies = []
    for c in range(C):
        arrived(fext, 1, c)
        re, im = apply(fext, c)
        anchor = vext[c, 2 * N : 3 * N, :].astype(f32)
        yall[0, c, :, 0:N] = (2.0 * re / FILTER_HALF - anchor[:, :N]).astype(bf16)
        yall[0, c, :, N : 2 * N] = (2.0 * im / FILTER_HALF - anchor[:, N:]).astype(bf16)
        y_copy(c, 1).start()
        y_copy(c, 0).start()
        for p in range(2):
            filt_copies.append(
                pltpu.make_async_copy(
                    yall.at[0, c, :, pl.ds(p * N, N)], filt_out.at[p, :, pl.ds(c * N, N)], filt_sem.at[c, p]
                )
            )
            filt_copies[-1].start()
    for c in range(C):
        add_rotated(0, c, k)
    for c in range(C):
        y = yall[0, c]
        y_re, y_im = y[:, :N], y[:, N:]
        left = jnp.concatenate(
            [jnp.concatenate([y_re, y_im], axis=1), jnp.concatenate([-y_im, y_re], axis=1)], axis=0
        )
        left_t[c] = jnp.transpose(left)
    for c in range(C):
        y_copy(c, 0).wait_recv()
        add_rotated(1, c, k1)
    for c in range(C):
        y_copy(c, 1).wait_recv()
        y_copy(c, 2).start()
        add_rotated(2, c, k2)
    for c in range(C):
        y_copy(c, 2).wait_recv()
        add_rotated(3, c, k3)

    for i in range(NX):
        rr[i] = racc[:, i * N : (i + 1) * N].astype(bf16)
    rot_copy = pltpu.make_async_copy(rr.at[k], rot_out, rot_sem.at[0])
    rot_copy.start()

    def rows_of(step_y):
        return pl.ds(pl.multiple_of(lax.rem(yi + step_y, NY) * 192, 64), 192)

    def x_copy(d, j):
        i = lax.rem(xi + d, NX)
        return remote(
            wsend.at[i, rows_of(j), :], recvx.at[d - 1, rows_of(j), :], x_ss.at[d - 1, j], x_rs.at[d - 1, j], x_peer(d), k
        )

    y_order = (2, 3, 1, 0)
    for d in (2, 1, 3, 0):
        i = lax.rem(xi + d, NX)
        panel = rr[i]
        for c in range(C):
            got = jnp.dot(left_t[c], panel, preferred_element_type=f32)
            for p in range(2):
                rows = slice(p * C * N + c * N, p * C * N + (c + 1) * N)
                if d == 0:
                    wacc[rows, :] = got[p * N : (p + 1) * N]
                else:
                    wsend[i, rows, :] = got[p * N : (p + 1) * N].astype(bf16)
        if d:
            for j in y_order:
                x_copy(d, j).start()

    def y2_copy(d):
        return remote(xsb.at[d], recvy.at[d - 1], x2_ss.at[d - 1], x2_rs.at[d - 1], y_peer(d), k)

    for j in y_order:
        for d in (1, 3, 2):
            x_copy(d, j).wait_recv()
        total = wacc[rows_of(j), :]
        for d in range(NX - 1):
            total = total + recvx[d, rows_of(j), :].astype(f32)
        if j:
            xsb[j] = total.astype(bf16)
            y2_copy(j).start()
        else:
            xs[...] = total

    for d in range(1, NY):
        y2_copy(d).wait_recv()
    total = xs[...]
    for d in range(NY - 1):
        total = total + recvy[d].astype(f32)
    ys[...] = total.reshape(NZ, 16, N)
    ysb[...] = total.astype(bf16).reshape(NZ, 16, N)

    def z_copy(d):
        return remote(ysb.at[lax.rem(zi + d, NZ)], recvz.at[d - 1], z_ss.at[d - 1], z_rs.at[d - 1], z_peer(d), k)

    far_first = (6, 5, 7, 4, 8, 3, 9, 2, 10, 1, 11)
    for d in far_first:
        z_copy(d).start()
    for d in range(1, NZ):
        z_copy(d).wait_recv()
    total = ys[zi]
    for d in range(NZ - 1):
        total = total + recvz[d].astype(f32)
    inverse_root = 1.0 / jnp.sqrt(jnp.float32(N * BLOCKS))

    def tile_of(step_z):
        return pl.ds(pl.multiple_of(yi * 192 + lax.rem(zi + step_z, NZ) * 16, 16), 16)

    ag[xi, tile_of(0), :] = (total * inverse_root).astype(bf16)

    def az_copy(d):
        piece = ag.at[xi, tile_of(0), :]
        return remote(piece, piece, az_ss.at[d - 1], az_rs.at[d - 1], z_peer(d), k)

    for d in far_first:
        az_copy(d).start()
    for d in range(1, NZ):
        az_copy(d).wait_recv()

    def ay_copy(d):
        piece = ag.at[xi, rows_of(0), :]
        return remote(piece, piece, ay_ss.at[d - 1], ay_rs.at[d - 1], y_peer(d), k)

    def ax_copy(d, j):
        piece = ag.at[xi, rows_of(NY - j), :]
        return remote(piece, piece, ax_ss.at[d - 1, j], ax_rs.at[d - 1, j], x_peer(d), k)

    for d in (2, 1, 3):
        ay_copy(d).start()
    for d in (2, 1, 3):
        ax_copy(d, 0).start()
    for j in (1, 3, 2):
        ay_copy(j).wait_recv()
        for d in (2, 1, 3):
            ax_copy(d, j).start()

    inter_copies = []
    for d in (0, 1, 3, 2):
        if d:
            for j in range(NY):
                ax_copy(d, j).wait_recv()
        i = lax.rem(xi + (NX - d), NX)
        for p in range(2):
            inter_copies.append(
                pltpu.make_async_copy(
                    ag.at[i, pl.ds(p * C * N, C * N), :],
                    inter_out.at[p, :, pl.ds(pl.multiple_of(i * N, N), N)],
                    inter_sem.at[d, p],
                )
            )
            inter_copies[-1].start()

    @pl.when(has_right)
    def _():
        pk_right.wait_send()

    @pl.when(has_left)
    def _():
        pk_left.wait_send()

    for rnd, buf in ((0, vext), (1, fext)):
        for c in range(C):
            @pl.when(has_right)
            def _():
                hop(buf, rnd, c, 0).wait_send()

            @pl.when(has_left)
            def _():
                hop(buf, rnd, c, 1).wait_send()

            @pl.when(has_left & has_right)
            def _():
                hop(buf, rnd, c, 2).wait_send()
                hop(buf, rnd, c, 3).wait_send()

    for c in range(C):
        for col in range(3):
            y_copy(c, col).wait_send()
    for d in range(1, NX):
        for j in range(NY):
            x_copy(d, j).wait_send()
            ax_copy(d, j).wait_send()
    for d in range(1, NY):
        y2_copy(d).wait_send()
        ay_copy(d).wait_send()
    for d in range(1, NZ):
        z_copy(d).wait_send()
        az_copy(d).wait_send()
    for copy in filt_copies + [rot_copy] + inter_copies:
        copy.wait()


def on_device(orbitals, elem_count, connectivity, elem_coef, elem_matrix, potential, absorber, rotation):
    f32, bf16 = jnp.float32, jnp.bfloat16
    hbm = pl.BlockSpec(memory_space=pl.ANY)
    vmem = pl.BlockSpec(memory_space=pltpu.VMEM)
    dma = pltpu.SemaphoreType.DMA
    filt, rotated, inter = pl.pallas_call(
        body,
        out_shape=(
            jax.ShapeDtypeStruct((2, N, C * N), bf16),
            jax.ShapeDtypeStruct((2 * N, N), bf16),
            jax.ShapeDtypeStruct((2, C * N, NX * N), bf16),
        ),
        in_specs=[hbm, vmem, vmem, vmem, vmem, vmem, vmem, hbm],
        out_specs=(hbm, hbm, hbm),
        scratch_shapes=[
            pltpu.VMEM((3, 8, JP), f32),
            pltpu.VMEM((JP, JP), bf16),
            pltpu.VMEM((2, N, N), f32),
            pltpu.VMEM((4 * JP, JP), bf16),
            pltpu.VMEM((4 * N, JP), bf16),
            pltpu.VMEM((2 * N, 4 * JP), bf16),
            pltpu.VMEM((N, 5 * N), f32),
            pltpu.VMEM((2 * N, 5 * N), bf16),
            pltpu.VMEM((N, 2, C * N), bf16),
            pltpu.VMEM((C, 5 * N, 2 * N), bf16),
            pltpu.VMEM((C, 5 * N, 2 * N), bf16),
            pltpu.VMEM((4 * C * N, 2, 4 * N), bf16),
            pltpu.VMEM((4 * C, 2 * N, 4 * N), bf16),
            pltpu.VMEM((4, C, N, 2 * N), bf16),
            pltpu.VMEM((C, 2 * N, 2 * N), bf16),
            pltpu.VMEM((2 * N, 4 * N), f32),
            pltpu.VMEM((4, 2 * N, N), bf16),
            pltpu.VMEM((6 * N, N), f32),
            pltpu.VMEM((NX, 6 * N, N), bf16),
            pltpu.VMEM((NX - 1, 6 * N, N), bf16),
            pltpu.VMEM((192, N), f32),
            pltpu.VMEM((NY, 192, N), bf16),
            pltpu.VMEM((NY - 1, 192, N), bf16),
            pltpu.VMEM((NZ, 16, N), f32),
            pltpu.VMEM((NZ, 16, N), bf16),
            pltpu.VMEM((NZ - 1, 16, N), bf16),
            pltpu.VMEM((NX, 6 * N, N), bf16),
            dma((1,)), dma((1,)), dma((C, 2)), dma((1,)), dma((NX, 2)),
            dma((2,)), dma((2,)),
            dma((2, C, 4)), dma((2, C, 4)),
            dma((C, 3)), dma((C, 3)),
            dma((NX - 1, NY)), dma((NX - 1, NY)),
            dma((NY - 1,)), dma((NY - 1,)),
            dma((NZ - 1,)), dma((NZ - 1,)),
            dma((NZ - 1,)), dma((NZ - 1,)),
            dma((NY - 1,)), dma((NY - 1,)),
            dma((NX - 1, NY)), dma((NX - 1, NY)),
        ],
        compiler_params=pltpu.CompilerParams(collective_id=0, has_side_effects=True, vmem_limit_bytes=66500000),
        name="filter_panel",
    )(
        orbitals, connectivity, elem_coef, elem_count.reshape(1, 1), elem_matrix,
        potential.reshape(1, N), absorber.reshape(1, N), rotation,
    )
    filtered = filt.transpose(1, 0, 2)
    rotated = rotated.reshape(2, N, N).transpose(1, 0, 2)
    return (filtered, rotated, inter.transpose(1, 0, 2).astype(f32))


def solution(mesh):
    placed = (
        P("elem", None, "band"),
        P("elem"),
        P("elem", None, None),
        P("elem", None),
        P(),
        P("elem"),
        P("elem"),
        P(),
    )
    return jax.shard_map(
        on_device,
        mesh=mesh,
        in_specs=placed,
        out_specs=(P("elem", None, "band"), P("elem", None, "band"), P("band", None, None)),
        check_vma=False,
    )
```

```python
import functools

import jax
import jax.numpy as jnp
from jax import lax
from jax.experimental import pallas as pl
from jax.experimental.pallas import tpu as pltpu
from jax.sharding import PartitionSpec as P

MESH = pl.DeviceIdType.MESH
FILTER_CENTER = 1.0
FILTER_HALF = 4.0

N = 128
C = 3
NX, NY, NZ = 4, 4, 12
BLOCKS = NX * NY * NZ
JP = 384
VMEM_LIMIT = 66500000
PREV, OWN, NEXT = 0, 1, 2


def body(
    orb, ids_hbm, coef_hbm, count_hbm, mat_hbm, pot_hbm, cap_hbm, rot, filt_out, rot_out, inter_out,
    ids_in, coef_in, count_in, mat_in, pot_in, cap_in, fin_f, fin_r, fin_i, pk, mat, diag, gall, gmine, both, sacc, s2, orb_raw, vext, fext, q_raw, qv, yall, left_t, racc, rr, wacc, wsend, recvx, xs, xsb,
    recvy, ys, ysb, recvz, ag,
    small_sem, orb_sem, q_sem, filt_sem, rot_sem, inter_sem, pk_ss, pk_rs, h_ss, h_rs, y_ss, y_rs, x_ss, x_rs,
    x2_ss, x2_rs, z_ss, z_rs, az_ss, az_rs, ay_ss, ay_rs, ax_ss, ax_rs,
):
    f32, bf16 = jnp.float32, jnp.bfloat16
    b = lax.axis_index("elem")
    k = lax.axis_index("band")
    xi = lax.rem(b, NX)
    yi = lax.rem(lax.div(b, NX), NY)
    zi = lax.div(b, NX * NY)
    k1 = k + 1 - 2 * lax.rem(k, 2)
    k2 = lax.rem(k + 2, 4)
    k3 = 3 - k
    has_left = b > 0
    has_right = b < BLOCKS - 1
    place = lax.rem(b, NX * NY)
    inner = (place > 0) & (place < NX * NY - 1)
    far_left = (place < 2) & (b > 1)
    far_right = (place > NX * NY - 3) & (b < BLOCKS - 2)

    def x_peer(d):
        return b - xi + lax.rem(xi + d, NX)

    def y_peer(d):
        return b + (lax.rem(yi + d, NY) - yi) * NX

    def z_peer(d):
        return b + (lax.rem(zi + d, NZ) - zi) * (NX * NY)

    barrier = pltpu.get_barrier_semaphore()

    def greet(e, kk):
        pl.semaphore_signal(barrier, inc=1, device_id=(e, kk), device_id_type=MESH)

    for d in range(1, NZ):
        greet(z_peer(d), k)

    @pl.when(has_left)
    def _():
        greet(b - 1, k)

    @pl.when(has_right)
    def _():
        greet(b + 1, k)

    @pl.when(far_left)
    def _():
        greet(b - 2, k)

    @pl.when(far_right)
    def _():
        greet(b + 2, k)

    greet(b, k2)
    for d in range(1, NY):
        greet(y_peer(d), k)
    for d in range(1, NX):
        greet(x_peer(d), k)
    greet(b, k1)

    load_orb = pltpu.make_async_copy(orb, orb_raw, orb_sem.at[0])
    load_orb.start()
    smalls = [
        pltpu.make_async_copy(src, dst, small_sem.at[i])
        for i, (src, dst) in enumerate(
            ((ids_hbm, ids_in), (coef_hbm, coef_in), (count_hbm, count_in), (pot_hbm, pot_in), (cap_hbm, cap_in), (mat_hbm, mat_in))
        )
    ]
    for load in smalls:
        load.start()
    load_q = pltpu.make_async_copy(rot, q_raw, q_sem.at[0])
    load_q.start()

    def clear(slot):
        zeros = jnp.zeros((C, N, 2 * N), bf16)
        vext[:, slot * N : (slot + 1) * N, :] = zeros
        fext[:, slot * N : (slot + 1) * N, :] = zeros

    @pl.when(b < 2)
    def _():
        clear(0)

    @pl.when(b < 1)
    def _():
        clear(1)
        pk[PREV] = jnp.zeros(pk.shape[1:], f32)

    @pl.when(b > BLOCKS - 3)
    def _():
        clear(4)

    @pl.when(b > BLOCKS - 2)
    def _():
        clear(3)
        pk[NEXT] = jnp.zeros(pk.shape[1:], f32)

    nodes = mat_in.shape[0]
    for load in smalls[:3]:
        load.wait()
    pk[OWN] = jnp.full(pk.shape[1:], -1.0, f32)
    pk[OWN, 0:4, 0:nodes] = ids_in[0].astype(f32)
    live = jnp.where(lax.broadcasted_iota(jnp.int32, (1, 4), 1) < count_in[0], coef_in[...], 0.0)
    for e in range(4):
        pk[OWN, 4 + e : 5 + e, :] = jnp.broadcast_to(live[:, e : e + 1], (1, JP))

    load_orb.wait()
    planes = jnp.swapaxes(orb_raw[...], 0, 1)
    for c in range(C):
        for p in range(2):
            vext[c, 2 * N : 3 * N, p * N : (p + 1) * N] = planes[p, :, c * N : (c + 1) * N]
    beside = sum(side.astype(jnp.int32) for side in (has_left, has_right, far_left, far_right))
    pl.semaphore_wait(barrier, 2 + NX - 1 + NY - 1 + NZ - 1 + beside)

    def remote(src, dst, ss, rs, e, kk):
        return pltpu.make_async_remote_copy(
            src_ref=src, dst_ref=dst, send_sem=ss, recv_sem=rs, device_id=(e, kk), device_id_type=MESH
        )

    def hop(buf, rnd, c, col):
        src_slot, dst_slot, step = ((2, 1, 1), (2, 3, -1), (1, 0, 1), (3, 4, -1), (2, 0, 2), (2, 4, -2))[col]
        return remote(
            buf.at[c, pl.ds(src_slot * N, N), :],
            buf.at[c, pl.ds(dst_slot * N, N), :],
            h_ss.at[rnd, c, col],
            h_rs.at[rnd, c, col if col < 4 else col - 2],
            b + step,
            k,
        )

    pk_right = remote(pk.at[OWN], pk.at[PREV], pk_ss.at[0], pk_rs.at[0], b + 1, k)
    pk_left = remote(pk.at[OWN], pk.at[NEXT], pk_ss.at[1], pk_rs.at[1], b - 1, k)

    @pl.when(has_right)
    def _():
        pk_right.start()

    @pl.when(has_left)
    def _():
        pk_left.start()

    def send_own(buf, rnd, c):
        @pl.when(has_right)
        def _():
            hop(buf, rnd, c, 0).start()

        @pl.when(has_left)
        def _():
            hop(buf, rnd, c, 1).start()

        @pl.when(far_right)
        def _():
            hop(buf, rnd, c, 4).start()

        @pl.when(far_left)
        def _():
            hop(buf, rnd, c, 5).start()

    def from_left(buf, rnd, c):
        @pl.when(has_left)
        def _():
            hop(buf, rnd, c, 0).wait_recv()

        @pl.when(inner)
        def _():
            hop(buf, rnd, c, 2).start()

    def from_right(buf, rnd, c):
        @pl.when(has_right)
        def _():
            hop(buf, rnd, c, 1).wait_recv()

        @pl.when(inner)
        def _():
            hop(buf, rnd, c, 3).start()

    def relay(buf, rnd, near, even, far):
        @pl.when(xi == 0)
        def _():
            for c in near:
                from_right(buf, rnd, c)
            for c in far:
                from_left(buf, rnd, c)

        @pl.when(xi == NX - 1)
        def _():
            for c in near:
                from_left(buf, rnd, c)
            for c in far:
                from_right(buf, rnd, c)

        @pl.when((xi > 0) & (xi < NX - 1))
        def _():
            for c in even:
                from_left(buf, rnd, c)
                from_right(buf, rnd, c)

    def arrived(buf, rnd, c):
        @pl.when(b > 1)
        def _():
            hop(buf, rnd, c, 2).wait_recv()

        @pl.when(b < BLOCKS - 2)
        def _():
            hop(buf, rnd, c, 3).wait_recv()

    for c in range(C):
        send_own(vext, 0, c)

    for load in smalls[3:]:
        load.wait()
    mat[...] = jnp.zeros(mat.shape, bf16)
    mat[0:nodes, 0:nodes] = mat_in[...]
    diag[0] = jnp.transpose(jnp.broadcast_to(pot_in[...], (N, N)))
    diag[1] = jnp.transpose(jnp.broadcast_to(cap_in[...], (N, N)))
    sacc[...] = jnp.zeros(sacc.shape, f32)

    def add_strip(which):
        rows = pk[which]
        columns = jnp.transpose(rows)
        lanes = lax.broadcasted_iota(jnp.int32, (JP, JP), 1).astype(f32)
        mine = (lax.broadcasted_iota(jnp.int32, (N, JP), 0) + (2 - which) * N).astype(f32)
        for e in range(4):
            gall[e * JP : (e + 1) * JP, :] = jnp.where(lanes == columns[:, e : e + 1], 1.0, 0.0).astype(bf16)
            gmine[e * N : (e + 1) * N, :] = jnp.where(mine == rows[e : e + 1, :], 1.0, 0.0).astype(bf16)
        part = jnp.dot(gmine[...], mat[...], preferred_element_type=f32)
        for e in range(4):
            term = part[e * N : (e + 1) * N] * rows[4 + e : 5 + e, :]
            high = term.astype(bf16)
            both[0:N, e * JP : (e + 1) * JP] = high
            both[N : 2 * N, e * JP : (e + 1) * JP] = (term - high.astype(f32)).astype(bf16)
        got = jnp.dot(both[...], gall[...], preferred_element_type=f32)
        cols = pl.ds(pl.multiple_of(which * N, N), JP)
        sacc[:, cols] = sacc[:, cols] + got[:N] + got[N:]

    def pack_from_left():
        @pl.when(has_left)
        def _():
            pk_right.wait_recv()

    def pack_from_right():
        @pl.when(has_right)
        def _():
            pk_left.wait_recv()

    add_strip(OWN)
    relay(vext, 0, (0, 1), (0,), ())
    right_first = xi == 0

    @pl.when(right_first)
    def _():
        pack_from_right()

    @pl.when(xi > 0)
    def _():
        pack_from_left()

    step = right_first.astype(jnp.int32)
    add_strip(2 * step)
    relay(vext, 0, (2,), (1,), ())

    @pl.when(right_first)
    def _():
        pack_from_left()

    @pl.when(xi > 0)
    def _():
        pack_from_right()

    add_strip(2 - 2 * step)
    relay(vext, 0, (), (2,), (0, 1, 2))

    high = sacc[...].astype(bf16)
    s2[0:N, :] = high
    s2[N : 2 * N, :] = (sacc[...] - high.astype(f32)).astype(bf16)

    def apply(buf, c):
        two = jnp.dot(s2[...], buf[c], preferred_element_type=f32)
        k_v = two[:N] + two[N:]
        own = buf[c, 2 * N : 3 * N, :].astype(f32)
        v_re, v_im = own[:, :N], own[:, N:]
        ham_re = k_v[:, :N] + diag[0] * v_re + diag[1] * v_im
        ham_im = k_v[:, N:] + diag[0] * v_im - diag[1] * v_re
        return (ham_re - FILTER_CENTER * v_re), (ham_im - FILTER_CENTER * v_im)

    def split_rotation(first, last):
        def one(i, carry):
            planes = jnp.swapaxes(q_raw[pl.ds(pl.multiple_of(i * N, N), N)], 0, 1)
            qv[i, 0:N, :] = planes[0]
            qv[i, N : 2 * N, :] = planes[1]
            return carry

        lax.fori_loop(first, last, one, 0)

    load_q.wait()
    split_rotation(0, 2 * C)
    for c in range(C):
        arrived(vext, 0, c)
        re, im = apply(vext, c)
        fext[c, 2 * N : 3 * N, 0:N] = (re / FILTER_HALF).astype(bf16)
        fext[c, 2 * N : 3 * N, N : 2 * N] = (im / FILTER_HALF).astype(bf16)
        send_own(fext, 1, c)
    split_rotation(2 * C, 4 * C)
    relay(fext, 1, (0, 1, 2), (0, 1, 2), (0, 1, 2))

    def y_copy(c, col):
        src, dst, kk = ((0, 1, k1), (0, 2, k2), (2, 3, k1))[col]
        return remote(yall.at[src, c], yall.at[dst, c], y_ss.at[c, col], y_rs.at[c, col], b, kk)

    def add_rotated(slot, c, kk):
        y = yall[slot, c]
        y_re, y_im = y[:, :N], y[:, N:]
        turned = jnp.concatenate(
            [jnp.concatenate([y_re, -y_im], axis=1), jnp.concatenate([y_im, y_re], axis=1)], axis=0
        )
        racc[...] = racc[...] + jnp.dot(turned, qv[kk * C + c], preferred_element_type=f32)

    racc[...] = jnp.zeros(racc.shape, f32)
    for c in range(C):
        arrived(fext, 1, c)
        re, im = apply(fext, c)
        anchor = vext[c, 2 * N : 3 * N, :].astype(f32)
        yall[0, c, :, 0:N] = (2.0 * re / FILTER_HALF - anchor[:, :N]).astype(bf16)
        yall[0, c, :, N : 2 * N] = (2.0 * im / FILTER_HALF - anchor[:, N:]).astype(bf16)
        y_copy(c, 1).start()
        y_copy(c, 0).start()
    for c in range(C):
        add_rotated(0, c, k)
    for c in range(C):
        y = yall[0, c]
        y_re, y_im = y[:, :N], y[:, N:]
        left = jnp.concatenate(
            [jnp.concatenate([y_re, y_im], axis=1), jnp.concatenate([-y_im, y_re], axis=1)], axis=0
        )
        left_t[c] = jnp.transpose(left)
        fin_f[:, :, c * N : (c + 1) * N] = jnp.swapaxes(jnp.stack([y_re, y_im], axis=0), 0, 1)
    filt_copy = pltpu.make_async_copy(fin_f, filt_out, filt_sem.at[0])
    filt_copy.start()
    for c in range(C):
        y_copy(c, 0).wait_recv()
        add_rotated(1, c, k1)
    for c in range(C):
        y_copy(c, 1).wait_recv()
        y_copy(c, 2).start()
        add_rotated(2, c, k2)
    for c in range(C):
        y_copy(c, 2).wait_recv()
        add_rotated(3, c, k3)

    for i in range(NX):
        rr[i] = racc[:, i * N : (i + 1) * N].astype(bf16)
    def rows_of(step_y):
        return pl.ds(pl.multiple_of(lax.rem(yi + step_y, NY) * 192, 64), 192)

    def x_copy(d, j):
        i = lax.rem(xi + d, NX)
        return remote(
            wsend.at[i, rows_of(j), :], recvx.at[d - 1, rows_of(j), :], x_ss.at[d - 1, j], x_rs.at[d - 1, j], x_peer(d), k
        )

    y_order = (2, 3, 1, 0)
    for d in (2, 1, 3, 0):
        i = lax.rem(xi + d, NX)
        panel = rr[i]
        for c in range(C):
            got = jnp.dot(left_t[c], panel, preferred_element_type=f32)
            for p in range(2):
                rows = slice(p * C * N + c * N, p * C * N + (c + 1) * N)
                if d == 0:
                    wacc[rows, :] = got[p * N : (p + 1) * N]
                else:
                    wsend[i, rows, :] = got[p * N : (p + 1) * N].astype(bf16)
        if d:
            for j in y_order:
                x_copy(d, j).start()

    fin_r[...] = jnp.swapaxes(rr[k].reshape(2, N, N), 0, 1)
    rot_copy = pltpu.make_async_copy(fin_r, rot_out, rot_sem.at[0])
    rot_copy.start()

    def y2_copy(d):
        return remote(xsb.at[d], recvy.at[d - 1], x2_ss.at[d - 1], x2_rs.at[d - 1], y_peer(d), k)

    for j in y_order:
        for d in (1, 3, 2):
            x_copy(d, j).wait_recv()
        total = wacc[rows_of(j), :]
        for d in range(NX - 1):
            total = total + recvx[d, rows_of(j), :].astype(f32)
        if j:
            xsb[j] = total.astype(bf16)
            y2_copy(j).start()
        else:
            xs[...] = total

    for d in range(1, NY):
        y2_copy(d).wait_recv()
    total = xs[...]
    for d in range(NY - 1):
        total = total + recvy[d].astype(f32)
    ys[...] = total.reshape(NZ, 16, N)
    ysb[...] = total.astype(bf16).reshape(NZ, 16, N)

    def z_copy(d):
        return remote(ysb.at[lax.rem(zi + d, NZ)], recvz.at[d - 1], z_ss.at[d - 1], z_rs.at[d - 1], z_peer(d), k)

    far_first = (6, 5, 7, 4, 8, 3, 9, 2, 10, 1, 11)
    for d in far_first:
        z_copy(d).start()
    for d in range(1, NZ):
        z_copy(d).wait_recv()
    total = ys[zi]
    for d in range(NZ - 1):
        total = total + recvz[d].astype(f32)
    inverse_root = 1.0 / jnp.sqrt(jnp.float32(N * BLOCKS))

    def tile_of(step_z):
        return pl.ds(pl.multiple_of(yi * 192 + lax.rem(zi + step_z, NZ) * 16, 16), 16)

    ag[xi, tile_of(0), :] = (total * inverse_root).astype(bf16)

    def az_copy(d):
        piece = ag.at[xi, tile_of(0), :]
        return remote(piece, piece, az_ss.at[d - 1], az_rs.at[d - 1], z_peer(d), k)

    for d in far_first:
        az_copy(d).start()
    for d in range(1, NZ):
        az_copy(d).wait_recv()

    def ay_copy(d):
        piece = ag.at[xi, rows_of(0), :]
        return remote(piece, piece, ay_ss.at[d - 1], ay_rs.at[d - 1], y_peer(d), k)

    def ax_copy(d, j):
        piece = ag.at[xi, rows_of(NY - j), :]
        return remote(piece, piece, ax_ss.at[d - 1, j], ax_rs.at[d - 1, j], x_peer(d), k)

    for d in (2, 1, 3):
        ay_copy(d).start()
    for d in (2, 1, 3):
        ax_copy(d, 0).start()
    for j in (1, 3, 2):
        ay_copy(j).wait_recv()
        for d in (2, 1, 3):
            ax_copy(d, j).start()

    inter_copies = []
    for d in (0, 1, 3, 2):
        if d:
            for j in range(NY):
                ax_copy(d, j).wait_recv()
        i = lax.rem(xi + (NX - d), NX)
        cols = pl.ds(pl.multiple_of(i * N, N), N)
        fin_i[:, :, cols] = jnp.swapaxes(ag[i].reshape(2, C * N, N), 0, 1).astype(f32)
        inter_copies.append(pltpu.make_async_copy(fin_i.at[:, :, cols], inter_out.at[:, :, cols], inter_sem.at[d]))
        inter_copies[-1].start()

    @pl.when(has_right)
    def _():
        pk_right.wait_send()

    @pl.when(has_left)
    def _():
        pk_left.wait_send()

    for rnd, buf in ((0, vext), (1, fext)):
        for c in range(C):
            @pl.when(has_right)
            def _():
                hop(buf, rnd, c, 0).wait_send()

            @pl.when(has_left)
            def _():
                hop(buf, rnd, c, 1).wait_send()

            @pl.when(inner)
            def _():
                hop(buf, rnd, c, 2).wait_send()
                hop(buf, rnd, c, 3).wait_send()

            @pl.when(far_right)
            def _():
                hop(buf, rnd, c, 4).wait_send()

            @pl.when(far_left)
            def _():
                hop(buf, rnd, c, 5).wait_send()

    for c in range(C):
        for col in range(3):
            y_copy(c, col).wait_send()
    for d in range(1, NX):
        for j in range(NY):
            x_copy(d, j).wait_send()
            ax_copy(d, j).wait_send()
    for d in range(1, NY):
        y2_copy(d).wait_send()
        ay_copy(d).wait_send()
    for d in range(1, NZ):
        z_copy(d).wait_send()
        az_copy(d).wait_send()
    for copy in [filt_copy, rot_copy] + inter_copies:
        copy.wait()


PARTS = 6


def write_out(filt, rot, inter, filt_out, rot_out, inter_out, filt_v, rot_v, inter_v, in_sem, out_sem):
    part = inter.shape[0] // PARTS
    trips = [(inter.at[rows], inter_v.at[rows], inter_out.at[rows]) for rows in (pl.ds(i * part, part) for i in range(PARTS))]
    trips += [(filt, filt_v, filt_out), (rot, rot_v, rot_out)]
    reads = [pltpu.make_async_copy(src, mid, in_sem.at[i]) for i, (src, mid, _) in enumerate(trips)]
    writes = [pltpu.make_async_copy(mid, dst, out_sem.at[i]) for i, (_, mid, dst) in enumerate(trips)]
    for read in reads:
        read.start()
    for read, write in zip(reads, writes):
        read.wait()
        write.start()
    for write in writes:
        write.wait()


def on_device(orbitals, elem_count, connectivity, elem_coef, elem_matrix, potential, absorber, rotation):
    f32, bf16 = jnp.float32, jnp.bfloat16
    anywhere = pl.BlockSpec(memory_space=pl.ANY)
    dma = pltpu.SemaphoreType.DMA
    results = pl.pallas_call(
        body,
        out_shape=(
            jax.ShapeDtypeStruct((N, 2, C * N), bf16),
            jax.ShapeDtypeStruct((N, 2, N), bf16),
            jax.ShapeDtypeStruct((C * N, 2, NX * N), f32),
        ),
        in_specs=[anywhere] * 8,
        out_specs=(anywhere, anywhere, anywhere),
        scratch_shapes=[
            pltpu.VMEM(connectivity.shape, jnp.int32),
            pltpu.VMEM(elem_coef.shape, f32),
            pltpu.SMEM((1,), jnp.int32),
            pltpu.VMEM(elem_matrix.shape, bf16),
            pltpu.VMEM((1, N), f32),
            pltpu.VMEM((1, N), f32),
            pltpu.VMEM((N, 2, C * N), bf16),
            pltpu.VMEM((N, 2, N), bf16),
            pltpu.VMEM((C * N, 2, NX * N), f32),
            pltpu.VMEM((3, 8, JP), f32),
            pltpu.VMEM((JP, JP), bf16),
            pltpu.VMEM((2, N, N), f32),
            pltpu.VMEM((4 * JP, JP), bf16),
            pltpu.VMEM((4 * N, JP), bf16),
            pltpu.VMEM((2 * N, 4 * JP), bf16),
            pltpu.VMEM((N, 5 * N), f32),
            pltpu.VMEM((2 * N, 5 * N), bf16),
            pltpu.VMEM((N, 2, C * N), bf16),
            pltpu.VMEM((C, 5 * N, 2 * N), bf16),
            pltpu.VMEM((C, 5 * N, 2 * N), bf16),
            pltpu.VMEM((4 * C * N, 2, 4 * N), bf16),
            pltpu.VMEM((4 * C, 2 * N, 4 * N), bf16),
            pltpu.VMEM((4, C, N, 2 * N), bf16),
            pltpu.VMEM((C, 2 * N, 2 * N), bf16),
            pltpu.VMEM((2 * N, 4 * N), f32),
            pltpu.VMEM((4, 2 * N, N), bf16),
            pltpu.VMEM((6 * N, N), f32),
            pltpu.VMEM((NX, 6 * N, N), bf16),
            pltpu.VMEM((NX - 1, 6 * N, N), bf16),
            pltpu.VMEM((192, N), f32),
            pltpu.VMEM((NY, 192, N), bf16),
            pltpu.VMEM((NY - 1, 192, N), bf16),
            pltpu.VMEM((NZ, 16, N), f32),
            pltpu.VMEM((NZ, 16, N), bf16),
            pltpu.VMEM((NZ - 1, 16, N), bf16),
            pltpu.VMEM((NX, 6 * N, N), bf16),
            dma((6,)), dma((1,)), dma((1,)), dma((1,)), dma((1,)), dma((NX,)),
            dma((2,)), dma((2,)),
            dma((2, C, 6)), dma((2, C, 4)),
            dma((C, 3)), dma((C, 3)),
            dma((NX - 1, NY)), dma((NX - 1, NY)),
            dma((NY - 1,)), dma((NY - 1,)),
            dma((NZ - 1,)), dma((NZ - 1,)),
            dma((NZ - 1,)), dma((NZ - 1,)),
            dma((NY - 1,)), dma((NY - 1,)),
            dma((NX - 1, NY)), dma((NX - 1, NY)),
        ],
        compiler_params=pltpu.CompilerParams(collective_id=0, has_side_effects=True, vmem_limit_bytes=VMEM_LIMIT),
        name="filter_panel",
    )(
        orbitals, connectivity, elem_coef, elem_count, elem_matrix,
        potential.reshape(1, N), absorber.reshape(1, N), rotation,
    )
    return pl.pallas_call(
        write_out,
        out_shape=tuple(jax.ShapeDtypeStruct(r.shape, r.dtype) for r in results),
        in_specs=[anywhere] * 3,
        out_specs=(anywhere,) * 3,
        scratch_shapes=[pltpu.VMEM(r.shape, r.dtype) for r in results] + [dma((PARTS + 2,)), dma((PARTS + 2,))],
        compiler_params=pltpu.CompilerParams(vmem_limit_bytes=VMEM_LIMIT),
        name="write_out",
    )(*results)


def solution(mesh):
    placed = (
        P("elem", None, "band"),
        P("elem"),
        P("elem", None, None),
        P("elem", None),
        P(),
        P("elem"),
        P("elem"),
        P(),
    )
    return jax.shard_map(
        on_device,
        mesh=mesh,
        in_specs=placed,
        out_specs=(P("elem", None, "band"), P("elem", None, "band"), P("band", None, None)),
        check_vma=False,
    )
```

```python
import functools

import jax
import jax.numpy as jnp
from jax import lax
from jax.experimental import pallas as pl
from jax.experimental.pallas import tpu as pltpu
from jax.sharding import PartitionSpec as P

MESH = pl.DeviceIdType.MESH
FILTER_CENTER = 1.0
FILTER_HALF = 4.0

N = 128
C = 3
NX, NY, NZ = 4, 4, 12
BLOCKS = NX * NY * NZ
JP = 384
VMEM_LIMIT = 66500000
PREV, OWN, NEXT = 0, 1, 2


def body(
    orb, ids_hbm, coef_hbm, count_hbm, mat_hbm, pot_hbm, cap_hbm, rot, filt_out, rot_out, inter_out,
    ids_in, coef_in, count_in, mat_in, pot_in, cap_in, pk, mat, diag, gall, gmine, both, sacc, s2, orb_raw, vext, fext, q_raw, qv, yall, left_t, racc, rr, wacc, wsend, recvx, xs, xsb,
    recvy, ys, ysb, recvz, ag,
    small_sem, orb_sem, q_sem, filt_sem, rot_sem, inter_sem, pk_ss, pk_rs, h_ss, h_rs, y_ss, y_rs, x_ss, x_rs,
    x2_ss, x2_rs, z_ss, z_rs, az_ss, az_rs, ay_ss, ay_rs, ax_ss, ax_rs,
):
    f32, bf16 = jnp.float32, jnp.bfloat16
    b = lax.axis_index("elem")
    k = lax.axis_index("band")
    xi = lax.rem(b, NX)
    yi = lax.rem(lax.div(b, NX), NY)
    zi = lax.div(b, NX * NY)
    k1 = k + 1 - 2 * lax.rem(k, 2)
    k2 = lax.rem(k + 2, 4)
    k3 = 3 - k
    has_left = b > 0
    has_right = b < BLOCKS - 1
    inner = has_left & has_right

    def x_peer(d):
        return b - xi + lax.rem(xi + d, NX)

    def y_peer(d):
        return b + (lax.rem(yi + d, NY) - yi) * NX

    def z_peer(d):
        return b + (lax.rem(zi + d, NZ) - zi) * (NX * NY)

    barrier = pltpu.get_barrier_semaphore()

    def greet(e, kk):
        pl.semaphore_signal(barrier, inc=1, device_id=(e, kk), device_id_type=MESH)

    for d in range(1, NZ):
        greet(z_peer(d), k)

    @pl.when(has_left)
    def _():
        greet(b - 1, k)

    @pl.when(has_right)
    def _():
        greet(b + 1, k)

    greet(b, k2)
    for d in range(1, NY):
        greet(y_peer(d), k)
    for d in range(1, NX):
        greet(x_peer(d), k)
    greet(b, k1)

    load_orb = pltpu.make_async_copy(orb, orb_raw, orb_sem.at[0])
    load_orb.start()
    smalls = [
        pltpu.make_async_copy(src, dst, small_sem.at[i])
        for i, (src, dst) in enumerate(
            ((ids_hbm, ids_in), (coef_hbm, coef_in), (count_hbm, count_in), (pot_hbm, pot_in), (cap_hbm, cap_in), (mat_hbm, mat_in))
        )
    ]
    for load in smalls:
        load.start()
    load_q = pltpu.make_async_copy(rot, q_raw, q_sem.at[0])
    load_q.start()

    def clear(slot):
        zeros = jnp.zeros((C, N, 2 * N), bf16)
        vext[:, slot * N : (slot + 1) * N, :] = zeros
        fext[:, slot * N : (slot + 1) * N, :] = zeros

    @pl.when(b < 2)
    def _():
        clear(0)

    @pl.when(b < 1)
    def _():
        clear(1)
        pk[PREV] = jnp.zeros(pk.shape[1:], f32)

    @pl.when(b > BLOCKS - 3)
    def _():
        clear(4)

    @pl.when(b > BLOCKS - 2)
    def _():
        clear(3)
        pk[NEXT] = jnp.zeros(pk.shape[1:], f32)

    nodes = mat_in.shape[0]
    for load in smalls[:3]:
        load.wait()
    pk[OWN] = jnp.full(pk.shape[1:], -1.0, f32)
    pk[OWN, 0:4, 0:nodes] = ids_in[0].astype(f32)
    live = jnp.where(lax.broadcasted_iota(jnp.int32, (1, 4), 1) < count_in[0], coef_in[...], 0.0)
    for e in range(4):
        pk[OWN, 4 + e : 5 + e, :] = jnp.broadcast_to(live[:, e : e + 1], (1, JP))

    load_orb.wait()
    planes = jnp.swapaxes(orb_raw[...], 0, 1)
    for c in range(C):
        for p in range(2):
            vext[c, 2 * N : 3 * N, p * N : (p + 1) * N] = planes[p, :, c * N : (c + 1) * N]
    beside = sum(side.astype(jnp.int32) for side in (has_left, has_right))
    pl.semaphore_wait(barrier, 2 + NX - 1 + NY - 1 + NZ - 1 + beside)

    def remote(src, dst, ss, rs, e, kk):
        return pltpu.make_async_remote_copy(
            src_ref=src, dst_ref=dst, send_sem=ss, recv_sem=rs, device_id=(e, kk), device_id_type=MESH
        )

    def hop(buf, rnd, c, col):
        src_slot, dst_slot, step = ((2, 1, 1), (2, 3, -1), (1, 0, 1), (3, 4, -1))[col]
        return remote(
            buf.at[c, pl.ds(src_slot * N, N), :],
            buf.at[c, pl.ds(dst_slot * N, N), :],
            h_ss.at[rnd, c, col],
            h_rs.at[rnd, c, col],
            b + step,
            k,
        )

    pk_right = remote(pk.at[OWN], pk.at[PREV], pk_ss.at[0], pk_rs.at[0], b + 1, k)
    pk_left = remote(pk.at[OWN], pk.at[NEXT], pk_ss.at[1], pk_rs.at[1], b - 1, k)

    @pl.when(has_right)
    def _():
        pk_right.start()

    @pl.when(has_left)
    def _():
        pk_left.start()

    def send_own(buf, rnd, c):
        @pl.when(has_right)
        def _():
            hop(buf, rnd, c, 0).start()

        @pl.when(has_left)
        def _():
            hop(buf, rnd, c, 1).start()

    def from_left(buf, rnd, c):
        @pl.when(has_left)
        def _():
            hop(buf, rnd, c, 0).wait_recv()

        @pl.when(inner)
        def _():
            hop(buf, rnd, c, 2).start()

    def from_right(buf, rnd, c):
        @pl.when(has_right)
        def _():
            hop(buf, rnd, c, 1).wait_recv()

        @pl.when(inner)
        def _():
            hop(buf, rnd, c, 3).start()

    def relay(buf, rnd, near, even, far):
        @pl.when(xi == 0)
        def _():
            for c in near:
                from_right(buf, rnd, c)
            for c in far:
                from_left(buf, rnd, c)

        @pl.when(xi == NX - 1)
        def _():
            for c in near:
                from_left(buf, rnd, c)
            for c in far:
                from_right(buf, rnd, c)

        @pl.when((xi > 0) & (xi < NX - 1))
        def _():
            for c in even:
                from_left(buf, rnd, c)
                from_right(buf, rnd, c)

    def arrived(buf, rnd, c):
        @pl.when(b > 1)
        def _():
            hop(buf, rnd, c, 2).wait_recv()

        @pl.when(b < BLOCKS - 2)
        def _():
            hop(buf, rnd, c, 3).wait_recv()

    for c in range(C):
        send_own(vext, 0, c)

    for load in smalls[3:]:
        load.wait()
    mat[...] = jnp.zeros(mat.shape, bf16)
    mat[0:nodes, 0:nodes] = mat_in[...]
    diag[0] = jnp.transpose(jnp.broadcast_to(pot_in[...], (N, N)))
    diag[1] = jnp.transpose(jnp.broadcast_to(cap_in[...], (N, N)))
    sacc[...] = jnp.zeros(sacc.shape, f32)

    def add_strip(which):
        rows = pk[which]
        columns = jnp.transpose(rows)
        lanes = lax.broadcasted_iota(jnp.int32, (JP, JP), 1).astype(f32)
        mine = (lax.broadcasted_iota(jnp.int32, (N, JP), 0) + (2 - which) * N).astype(f32)
        for e in range(4):
            gall[e * JP : (e + 1) * JP, :] = jnp.where(lanes == columns[:, e : e + 1], 1.0, 0.0).astype(bf16)
            gmine[e * N : (e + 1) * N, :] = jnp.where(mine == rows[e : e + 1, :], 1.0, 0.0).astype(bf16)
        part = jnp.dot(gmine[...], mat[...], preferred_element_type=f32)
        for e in range(4):
            term = part[e * N : (e + 1) * N] * rows[4 + e : 5 + e, :]
            high = term.astype(bf16)
            both[0:N, e * JP : (e + 1) * JP] = high
            both[N : 2 * N, e * JP : (e + 1) * JP] = (term - high.astype(f32)).astype(bf16)
        got = jnp.dot(both[...], gall[...], preferred_element_type=f32)
        cols = pl.ds(pl.multiple_of(which * N, N), JP)
        sacc[:, cols] = sacc[:, cols] + got[:N] + got[N:]

    def pack_from_left():
        @pl.when(has_left)
        def _():
            pk_right.wait_recv()

    def pack_from_right():
        @pl.when(has_right)
        def _():
            pk_left.wait_recv()

    add_strip(OWN)
    relay(vext, 0, (0, 1), (0,), ())
    right_first = xi == 0

    @pl.when(right_first)
    def _():
        pack_from_right()

    @pl.when(xi > 0)
    def _():
        pack_from_left()

    step = right_first.astype(jnp.int32)
    add_strip(2 * step)
    relay(vext, 0, (2,), (1,), ())

    @pl.when(right_first)
    def _():
        pack_from_left()

    @pl.when(xi > 0)
    def _():
        pack_from_right()

    add_strip(2 - 2 * step)
    relay(vext, 0, (), (2,), (0, 1, 2))

    high = sacc[...].astype(bf16)
    s2[0:N, :] = high
    s2[N : 2 * N, :] = (sacc[...] - high.astype(f32)).astype(bf16)

    def apply(buf, c):
        two = jnp.dot(s2[...], buf[c], preferred_element_type=f32)
        k_v = two[:N] + two[N:]
        own = buf[c, 2 * N : 3 * N, :].astype(f32)
        v_re, v_im = own[:, :N], own[:, N:]
        ham_re = k_v[:, :N] + diag[0] * v_re + diag[1] * v_im
        ham_im = k_v[:, N:] + diag[0] * v_im - diag[1] * v_re
        return (ham_re - FILTER_CENTER * v_re), (ham_im - FILTER_CENTER * v_im)

    def split_rotation(first, last):
        def one(i, carry):
            planes = jnp.swapaxes(q_raw[pl.ds(pl.multiple_of(i * N, N), N)], 0, 1)
            qv[i, 0:N, :] = planes[0]
            qv[i, N : 2 * N, :] = planes[1]
            return carry

        lax.fori_loop(first, last, one, 0)

    load_q.wait()
    split_rotation(0, 2 * C)
    for c in range(C):
        arrived(vext, 0, c)
        re, im = apply(vext, c)
        fext[c, 2 * N : 3 * N, 0:N] = (re / FILTER_HALF).astype(bf16)
        fext[c, 2 * N : 3 * N, N : 2 * N] = (im / FILTER_HALF).astype(bf16)
        send_own(fext, 1, c)
    split_rotation(2 * C, 4 * C)
    relay(fext, 1, (0, 1, 2), (0, 1, 2), (0, 1, 2))

    def y_copy(c, col):
        src, dst, kk = ((0, 1, k1), (0, 2, k2), (2, 3, k1))[col]
        return remote(yall.at[src, c], yall.at[dst, c], y_ss.at[c, col], y_rs.at[c, col], b, kk)

    def add_rotated(slot, c, kk):
        y = yall[slot, c]
        y_re, y_im = y[:, :N], y[:, N:]
        turned = jnp.concatenate(
            [jnp.concatenate([y_re, -y_im], axis=1), jnp.concatenate([y_im, y_re], axis=1)], axis=0
        )
        racc[...] = racc[...] + jnp.dot(turned, qv[kk * C + c], preferred_element_type=f32)

    racc[...] = jnp.zeros(racc.shape, f32)
    for c in range(C):
        arrived(fext, 1, c)
        re, im = apply(fext, c)
        anchor = vext[c, 2 * N : 3 * N, :].astype(f32)
        yall[0, c, :, 0:N] = (2.0 * re / FILTER_HALF - anchor[:, :N]).astype(bf16)
        yall[0, c, :, N : 2 * N] = (2.0 * im / FILTER_HALF - anchor[:, N:]).astype(bf16)
        y_copy(c, 1).start()
        y_copy(c, 0).start()
    for c in range(C):
        add_rotated(0, c, k)
    for c in range(C):
        y = yall[0, c]
        y_re, y_im = y[:, :N], y[:, N:]
        left = jnp.concatenate(
            [jnp.concatenate([y_re, y_im], axis=1), jnp.concatenate([-y_im, y_re], axis=1)], axis=0
        )
        left_t[c] = jnp.transpose(left)
    filt_copy = pltpu.make_async_copy(yall.at[0], filt_out, filt_sem.at[0])
    filt_copy.start()
    for c in range(C):
        y_copy(c, 0).wait_recv()
        add_rotated(1, c, k1)
    for c in range(C):
        y_copy(c, 1).wait_recv()
        y_copy(c, 2).start()
        add_rotated(2, c, k2)
    for c in range(C):
        y_copy(c, 2).wait_recv()
        add_rotated(3, c, k3)

    for i in range(NX):
        rr[i] = racc[:, i * N : (i + 1) * N].astype(bf16)
    def rows_of(step_y):
        return pl.ds(pl.multiple_of(lax.rem(yi + step_y, NY) * 192, 64), 192)

    def x_copy(d, j):
        i = lax.rem(xi + d, NX)
        return remote(
            wsend.at[i, rows_of(j), :], recvx.at[d - 1, rows_of(j), :], x_ss.at[d - 1, j], x_rs.at[d - 1, j], x_peer(d), k
        )

    y_order = (2, 3, 1, 0)
    for d in (1, 3, 2, 0):
        i = lax.rem(xi + d, NX)
        panel = rr[i]
        for c in range(C):
            got = jnp.dot(left_t[c], panel, preferred_element_type=f32)
            for p in range(2):
                rows = slice(p * C * N + c * N, p * C * N + (c + 1) * N)
                if d == 0:
                    wacc[rows, :] = got[p * N : (p + 1) * N]
                else:
                    wsend[i, rows, :] = got[p * N : (p + 1) * N].astype(bf16)
        if d:
            for j in y_order:
                x_copy(d, j).start()

    rot_copy = pltpu.make_async_copy(rr.at[k], rot_out, rot_sem.at[0])
    rot_copy.start()

    def y2_copy(d):
        return remote(xsb.at[d], recvy.at[d - 1], x2_ss.at[d - 1], x2_rs.at[d - 1], y_peer(d), k)

    for j in y_order:
        for d in (1, 3, 2):
            x_copy(d, j).wait_recv()
        total = wacc[rows_of(j), :]
        for d in range(NX - 1):
            total = total + recvx[d, rows_of(j), :].astype(f32)
        if j:
            xsb[j] = total.astype(bf16)
            y2_copy(j).start()
        else:
            xs[...] = total

    for d in range(1, NY):
        y2_copy(d).wait_recv()
    total = xs[...]
    for d in range(NY - 1):
        total = total + recvy[d].astype(f32)
    ys[...] = total.reshape(NZ, 16, N)
    ysb[...] = total.astype(bf16).reshape(NZ, 16, N)

    def z_copy(d):
        return remote(ysb.at[lax.rem(zi + d, NZ)], recvz.at[d - 1], z_ss.at[d - 1], z_rs.at[d - 1], z_peer(d), k)

    far_first = (6, 5, 7, 4, 8, 3, 9, 2, 10, 1, 11)
    for d in far_first:
        z_copy(d).start()
    for d in range(1, NZ):
        z_copy(d).wait_recv()
    total = ys[zi]
    for d in range(NZ - 1):
        total = total + recvz[d].astype(f32)
    inverse_root = 1.0 / jnp.sqrt(jnp.float32(N * BLOCKS))

    def tile_of(step_z):
        return pl.ds(pl.multiple_of(yi * 192 + lax.rem(zi + step_z, NZ) * 16, 16), 16)

    ag[xi, tile_of(0), :] = (total * inverse_root).astype(bf16)

    def az_copy(d):
        piece = ag.at[xi, tile_of(0), :]
        return remote(piece, piece, az_ss.at[d - 1], az_rs.at[d - 1], z_peer(d), k)

    for d in far_first:
        az_copy(d).start()
    for d in range(1, NZ):
        az_copy(d).wait_recv()

    def ay_copy(d):
        piece = ag.at[xi, rows_of(0), :]
        return remote(piece, piece, ay_ss.at[d - 1], ay_rs.at[d - 1], y_peer(d), k)

    def ax_copy(d, j):
        piece = ag.at[xi, rows_of(NY - j), :]
        return remote(piece, piece, ax_ss.at[d - 1, j], ax_rs.at[d - 1, j], x_peer(d), k)

    for d in (2, 1, 3):
        ay_copy(d).start()
    for d in (1, 3, 2):
        ax_copy(d, 0).start()
    for j in (1, 3, 2):
        ay_copy(j).wait_recv()
        for d in (1, 3, 2):
            ax_copy(d, j).start()

    inter_copies = []
    for d in (0, 1, 3, 2):
        if d:
            for j in range(NY):
                ax_copy(d, j).wait_recv()
        i = lax.rem(xi + (NX - d), NX)
        inter_copies.append(pltpu.make_async_copy(ag.at[i], inter_out.at[i], inter_sem.at[d]))
        inter_copies[-1].start()

    @pl.when(has_right)
    def _():
        pk_right.wait_send()

    @pl.when(has_left)
    def _():
        pk_left.wait_send()

    for rnd, buf in ((0, vext), (1, fext)):
        for c in range(C):
            @pl.when(has_right)
            def _():
                hop(buf, rnd, c, 0).wait_send()

            @pl.when(has_left)
            def _():
                hop(buf, rnd, c, 1).wait_send()

            @pl.when(inner)
            def _():
                hop(buf, rnd, c, 2).wait_send()
                hop(buf, rnd, c, 3).wait_send()

    for c in range(C):
        for col in range(3):
            y_copy(c, col).wait_send()
    for d in range(1, NX):
        for j in range(NY):
            x_copy(d, j).wait_send()
            ax_copy(d, j).wait_send()
    for d in range(1, NY):
        y2_copy(d).wait_send()
        ay_copy(d).wait_send()
    for d in range(1, NZ):
        z_copy(d).wait_send()
        az_copy(d).wait_send()
    for copy in [filt_copy, rot_copy] + inter_copies:
        copy.wait()


def write_out(filt, rot, inter, filt_out, rot_out, inter_out, filt_v, rot_v, inter_v, filt_f, rot_f, inter_f, in_sem, out_sem):
    reads = [pltpu.make_async_copy(filt, filt_v, in_sem.at[0]), pltpu.make_async_copy(rot, rot_v, in_sem.at[1])]
    reads += [pltpu.make_async_copy(inter.at[i], inter_v.at[i], in_sem.at[2 + i]) for i in range(NX)]
    writes = [pltpu.make_async_copy(filt_f, filt_out, out_sem.at[0]), pltpu.make_async_copy(rot_f, rot_out, out_sem.at[1])]
    for read in reads[2:] + reads[:2]:
        read.start()
    for i in range(NX):
        reads[2 + i].wait()
        inter_f[i] = inter_v[i].astype(jnp.float32)
        for p in range(2):
            writes.append(
                pltpu.make_async_copy(
                    inter_f.at[i, pl.ds(p * C * N, C * N), :],
                    inter_out.at[:, p, pl.ds(i * N, N)],
                    out_sem.at[2 + 2 * i + p],
                )
            )
            writes[-1].start()
    reads[0].wait()
    for c in range(C):
        y = filt_v[c]
        filt_f[:, :, c * N : (c + 1) * N] = jnp.swapaxes(jnp.stack([y[:, :N], y[:, N:]], axis=0), 0, 1)
    writes[0].start()
    reads[1].wait()
    rot_f[...] = jnp.swapaxes(rot_v[...].reshape(2, N, N), 0, 1)
    writes[1].start()
    for write in writes:
        write.wait()


def on_device(orbitals, elem_count, connectivity, elem_coef, elem_matrix, potential, absorber, rotation):
    f32, bf16 = jnp.float32, jnp.bfloat16
    anywhere = pl.BlockSpec(memory_space=pl.ANY)
    dma = pltpu.SemaphoreType.DMA
    results = pl.pallas_call(
        body,
        out_shape=(
            jax.ShapeDtypeStruct((C, N, 2 * N), bf16),
            jax.ShapeDtypeStruct((2 * N, N), bf16),
            jax.ShapeDtypeStruct((NX, 6 * N, N), bf16),
        ),
        in_specs=[anywhere] * 8,
        out_specs=(anywhere, anywhere, anywhere),
        scratch_shapes=[
            pltpu.VMEM(connectivity.shape, jnp.int32),
            pltpu.VMEM(elem_coef.shape, f32),
            pltpu.SMEM((1,), jnp.int32),
            pltpu.VMEM(elem_matrix.shape, bf16),
            pltpu.VMEM((1, N), f32),
            pltpu.VMEM((1, N), f32),
            pltpu.VMEM((3, 8, JP), f32),
            pltpu.VMEM((JP, JP), bf16),
            pltpu.VMEM((2, N, N), f32),
            pltpu.VMEM((4 * JP, JP), bf16),
            pltpu.VMEM((4 * N, JP), bf16),
            pltpu.VMEM((2 * N, 4 * JP), bf16),
            pltpu.VMEM((N, 5 * N), f32),
            pltpu.VMEM((2 * N, 5 * N), bf16),
            pltpu.VMEM((N, 2, C * N), bf16),
            pltpu.VMEM((C, 5 * N, 2 * N), bf16),
            pltpu.VMEM((C, 5 * N, 2 * N), bf16),
            pltpu.VMEM((4 * C * N, 2, 4 * N), bf16),
            pltpu.VMEM((4 * C, 2 * N, 4 * N), bf16),
            pltpu.VMEM((4, C, N, 2 * N), bf16),
            pltpu.VMEM((C, 2 * N, 2 * N), bf16),
            pltpu.VMEM((2 * N, 4 * N), f32),
            pltpu.VMEM((4, 2 * N, N), bf16),
            pltpu.VMEM((6 * N, N), f32),
            pltpu.VMEM((NX, 6 * N, N), bf16),
            pltpu.VMEM((NX - 1, 6 * N, N), bf16),
            pltpu.VMEM((192, N), f32),
            pltpu.VMEM((NY, 192, N), bf16),
            pltpu.VMEM((NY - 1, 192, N), bf16),
            pltpu.VMEM((NZ, 16, N), f32),
            pltpu.VMEM((NZ, 16, N), bf16),
            pltpu.VMEM((NZ - 1, 16, N), bf16),
            pltpu.VMEM((NX, 6 * N, N), bf16),
            dma((6,)), dma((1,)), dma((1,)), dma((1,)), dma((1,)), dma((NX,)),
            dma((2,)), dma((2,)),
            dma((2, C, 4)), dma((2, C, 4)),
            dma((C, 3)), dma((C, 3)),
            dma((NX - 1, NY)), dma((NX - 1, NY)),
            dma((NY - 1,)), dma((NY - 1,)),
            dma((NZ - 1,)), dma((NZ - 1,)),
            dma((NZ - 1,)), dma((NZ - 1,)),
            dma((NY - 1,)), dma((NY - 1,)),
            dma((NX - 1, NY)), dma((NX - 1, NY)),
        ],
        compiler_params=pltpu.CompilerParams(collective_id=0, has_side_effects=True, vmem_limit_bytes=VMEM_LIMIT),
        name="filter_panel",
    )(
        orbitals, connectivity, elem_coef, elem_count, elem_matrix,
        potential.reshape(1, N), absorber.reshape(1, N), rotation,
    )
    outs = ((N, 2, C * N), (N, 2, N), (C * N, 2, NX * N))
    return pl.pallas_call(
        write_out,
        out_shape=tuple(jax.ShapeDtypeStruct(shape, kind) for shape, kind in zip(outs, (bf16, bf16, f32))),
        in_specs=[anywhere] * 3,
        out_specs=(anywhere,) * 3,
        scratch_shapes=[pltpu.VMEM(r.shape, r.dtype) for r in results]
        + [pltpu.VMEM(outs[0], bf16), pltpu.VMEM(outs[1], bf16), pltpu.VMEM((NX, 6 * N, N), f32), dma((6,)), dma((10,))],
        compiler_params=pltpu.CompilerParams(vmem_limit_bytes=VMEM_LIMIT),
        name="write_out",
    )(*results)


def solution(mesh):
    placed = (
        P("elem", None, "band"),
        P("elem"),
        P("elem", None, None),
        P("elem", None),
        P(),
        P("elem"),
        P("elem"),
        P(),
    )
    return jax.shard_map(
        on_device,
        mesh=mesh,
        in_specs=placed,
        out_specs=(P("elem", None, "band"), P("elem", None, "band"), P("band", None, None)),
        check_vma=False,
    )
```

```python
import functools

import jax
import jax.numpy as jnp
from jax import lax
from jax.experimental import pallas as pl
from jax.experimental.pallas import tpu as pltpu
from jax.sharding import PartitionSpec as P

MESH = pl.DeviceIdType.MESH
FILTER_CENTER = 1.0
FILTER_HALF = 4.0

N = 128
C = 3
NX, NY, NZ = 4, 4, 12
BLOCKS = NX * NY * NZ
JP = 384
VMEM_LIMIT = 66500000
AT = 9
AR = AT * 16
BR = (NZ - AT) * 16
PREV, OWN, NEXT = 0, 1, 2


def body(
    orb, ids_hbm, coef_hbm, count_hbm, mat_hbm, pot_hbm, cap_hbm, rot, filt_out, rot_out, inter_out,
    ids_in, coef_in, count_in, mat_in, pot_in, cap_in, pk, mat, diag, gall, gmine, both, sacc, s2, orb_raw, vext, fext, q_raw, qv, yall, left_t, racc, rr, wacc, wsend, recvx, xs, xsb,
    recvy, recvb, ysend, ysb_own, recvbx, ys, ysb, recvz, ag,
    small_sem, orb_sem, q_sem, filt_sem, rot_sem, inter_sem, pk_ss, pk_rs, h_ss, h_rs, y_ss, y_rs, x_ss, x_rs,
    x2_ss, x2_rs, z_ss, z_rs, az_ss, az_rs, ay_ss, ay_rs, ax_ss, ax_rs,
    by_ss, by_rs, bx_ss, bx_rs, cx_ss, cx_rs, cy_ss, cy_rs,
):
    f32, bf16 = jnp.float32, jnp.bfloat16
    b = lax.axis_index("elem")
    k = lax.axis_index("band")
    xi = lax.rem(b, NX)
    yi = lax.rem(lax.div(b, NX), NY)
    zi = lax.div(b, NX * NY)
    k1 = k + 1 - 2 * lax.rem(k, 2)
    k2 = lax.rem(k + 2, 4)
    k3 = 3 - k
    has_left = b > 0
    has_right = b < BLOCKS - 1
    inner = has_left & has_right

    def x_peer(d):
        return b - xi + lax.rem(xi + d, NX)

    def y_peer(d):
        return b + (lax.rem(yi + d, NY) - yi) * NX

    def z_peer(d):
        return b + (lax.rem(zi + d, NZ) - zi) * (NX * NY)

    barrier = pltpu.get_barrier_semaphore()

    def greet(e, kk):
        pl.semaphore_signal(barrier, inc=1, device_id=(e, kk), device_id_type=MESH)

    for d in range(1, NZ):
        greet(z_peer(d), k)

    @pl.when(has_left)
    def _():
        greet(b - 1, k)

    @pl.when(has_right)
    def _():
        greet(b + 1, k)

    greet(b, k2)
    for d in range(1, NY):
        greet(y_peer(d), k)
    for d in range(1, NX):
        greet(x_peer(d), k)
    greet(b, k1)

    load_orb = pltpu.make_async_copy(orb, orb_raw, orb_sem.at[0])
    load_orb.start()
    smalls = [
        pltpu.make_async_copy(src, dst, small_sem.at[i])
        for i, (src, dst) in enumerate(
            ((ids_hbm, ids_in), (coef_hbm, coef_in), (count_hbm, count_in), (pot_hbm, pot_in), (cap_hbm, cap_in), (mat_hbm, mat_in))
        )
    ]
    for load in smalls:
        load.start()
    load_q = pltpu.make_async_copy(rot, q_raw, q_sem.at[0])
    load_q.start()

    def clear(slot):
        zeros = jnp.zeros((C, N, 2 * N), bf16)
        vext[:, slot * N : (slot + 1) * N, :] = zeros
        fext[:, slot * N : (slot + 1) * N, :] = zeros

    @pl.when(b < 2)
    def _():
        clear(0)

    @pl.when(b < 1)
    def _():
        clear(1)
        pk[PREV] = jnp.zeros(pk.shape[1:], f32)

    @pl.when(b > BLOCKS - 3)
    def _():
        clear(4)

    @pl.when(b > BLOCKS - 2)
    def _():
        clear(3)
        pk[NEXT] = jnp.zeros(pk.shape[1:], f32)

    nodes = mat_in.shape[0]
    for load in smalls[:3]:
        load.wait()
    pk[OWN] = jnp.full(pk.shape[1:], -1.0, f32)
    pk[OWN, 0:4, 0:nodes] = ids_in[0].astype(f32)
    live = jnp.where(lax.broadcasted_iota(jnp.int32, (1, 4), 1) < count_in[0], coef_in[...], 0.0)
    for e in range(4):
        pk[OWN, 4 + e : 5 + e, :] = jnp.broadcast_to(live[:, e : e + 1], (1, JP))

    load_orb.wait()
    planes = jnp.swapaxes(orb_raw[...], 0, 1)
    for c in range(C):
        for p in range(2):
            vext[c, 2 * N : 3 * N, p * N : (p + 1) * N] = planes[p, :, c * N : (c + 1) * N]
    beside = sum(side.astype(jnp.int32) for side in (has_left, has_right))
    pl.semaphore_wait(barrier, 2 + NX - 1 + NY - 1 + NZ - 1 + beside)

    def remote(src, dst, ss, rs, e, kk):
        return pltpu.make_async_remote_copy(
            src_ref=src, dst_ref=dst, send_sem=ss, recv_sem=rs, device_id=(e, kk), device_id_type=MESH
        )

    def hop(buf, rnd, c, col):
        src_slot, dst_slot, step = ((2, 1, 1), (2, 3, -1), (1, 0, 1), (3, 4, -1))[col]
        return remote(
            buf.at[c, pl.ds(src_slot * N, N), :],
            buf.at[c, pl.ds(dst_slot * N, N), :],
            h_ss.at[rnd, c, col],
            h_rs.at[rnd, c, col],
            b + step,
            k,
        )

    pk_right = remote(pk.at[OWN], pk.at[PREV], pk_ss.at[0], pk_rs.at[0], b + 1, k)
    pk_left = remote(pk.at[OWN], pk.at[NEXT], pk_ss.at[1], pk_rs.at[1], b - 1, k)

    @pl.when(has_right)
    def _():
        pk_right.start()

    @pl.when(has_left)
    def _():
        pk_left.start()

    def send_own(buf, rnd, c):
        @pl.when(has_right)
        def _():
            hop(buf, rnd, c, 0).start()

        @pl.when(has_left)
        def _():
            hop(buf, rnd, c, 1).start()

    def from_left(buf, rnd, c):
        @pl.when(has_left)
        def _():
            hop(buf, rnd, c, 0).wait_recv()

        @pl.when(inner)
        def _():
            hop(buf, rnd, c, 2).start()

    def from_right(buf, rnd, c):
        @pl.when(has_right)
        def _():
            hop(buf, rnd, c, 1).wait_recv()

        @pl.when(inner)
        def _():
            hop(buf, rnd, c, 3).start()

    def relay(buf, rnd, near, even, far):
        @pl.when(xi == 0)
        def _():
            for c in near:
                from_right(buf, rnd, c)
            for c in far:
                from_left(buf, rnd, c)

        @pl.when(xi == NX - 1)
        def _():
            for c in near:
                from_left(buf, rnd, c)
            for c in far:
                from_right(buf, rnd, c)

        @pl.when((xi > 0) & (xi < NX - 1))
        def _():
            for c in even:
                from_left(buf, rnd, c)
                from_right(buf, rnd, c)

    def arrived(buf, rnd, c):
        @pl.when(b > 1)
        def _():
            hop(buf, rnd, c, 2).wait_recv()

        @pl.when(b < BLOCKS - 2)
        def _():
            hop(buf, rnd, c, 3).wait_recv()

    for c in range(C):
        send_own(vext, 0, c)

    for load in smalls[3:]:
        load.wait()
    mat[...] = jnp.zeros(mat.shape, bf16)
    mat[0:nodes, 0:nodes] = mat_in[...]
    diag[0] = jnp.transpose(jnp.broadcast_to(pot_in[...], (N, N)))
    diag[1] = jnp.transpose(jnp.broadcast_to(cap_in[...], (N, N)))
    sacc[...] = jnp.zeros(sacc.shape, f32)

    def add_strip(which):
        rows = pk[which]
        columns = jnp.transpose(rows)
        lanes = lax.broadcasted_iota(jnp.int32, (JP, JP), 1).astype(f32)
        mine = (lax.broadcasted_iota(jnp.int32, (N, JP), 0) + (2 - which) * N).astype(f32)
        for e in range(4):
            gall[e * JP : (e + 1) * JP, :] = jnp.where(lanes == columns[:, e : e + 1], 1.0, 0.0).astype(bf16)
            gmine[e * N : (e + 1) * N, :] = jnp.where(mine == rows[e : e + 1, :], 1.0, 0.0).astype(bf16)
        part = jnp.dot(gmine[...], mat[...], preferred_element_type=f32)
        for e in range(4):
            term = part[e * N : (e + 1) * N] * rows[4 + e : 5 + e, :]
            high = term.astype(bf16)
            both[0:N, e * JP : (e + 1) * JP] = high
            both[N : 2 * N, e * JP : (e + 1) * JP] = (term - high.astype(f32)).astype(bf16)
        got = jnp.dot(both[...], gall[...], preferred_element_type=f32)
        cols = pl.ds(pl.multiple_of(which * N, N), JP)
        sacc[:, cols] = sacc[:, cols] + got[:N] + got[N:]

    def pack_from_left():
        @pl.when(has_left)
        def _():
            pk_right.wait_recv()

    def pack_from_right():
        @pl.when(has_right)
        def _():
            pk_left.wait_recv()

    add_strip(OWN)
    relay(vext, 0, (0, 1), (0,), ())
    right_first = xi == 0

    @pl.when(right_first)
    def _():
        pack_from_right()

    @pl.when(xi > 0)
    def _():
        pack_from_left()

    step = right_first.astype(jnp.int32)
    add_strip(2 * step)
    relay(vext, 0, (2,), (1,), ())

    @pl.when(right_first)
    def _():
        pack_from_left()

    @pl.when(xi > 0)
    def _():
        pack_from_right()

    add_strip(2 - 2 * step)
    relay(vext, 0, (), (2,), (0, 1, 2))

    high = sacc[...].astype(bf16)
    s2[0:N, :] = high
    s2[N : 2 * N, :] = (sacc[...] - high.astype(f32)).astype(bf16)

    def apply(buf, c):
        two = jnp.dot(s2[...], buf[c], preferred_element_type=f32)
        k_v = two[:N] + two[N:]
        own = buf[c, 2 * N : 3 * N, :].astype(f32)
        v_re, v_im = own[:, :N], own[:, N:]
        ham_re = k_v[:, :N] + diag[0] * v_re + diag[1] * v_im
        ham_im = k_v[:, N:] + diag[0] * v_im - diag[1] * v_re
        return (ham_re - FILTER_CENTER * v_re), (ham_im - FILTER_CENTER * v_im)

    def split_rotation(first, last):
        def one(i, carry):
            planes = jnp.swapaxes(q_raw[pl.ds(pl.multiple_of(i * N, N), N)], 0, 1)
            qv[i, 0:N, :] = planes[0]
            qv[i, N : 2 * N, :] = planes[1]
            return carry

        lax.fori_loop(first, last, one, 0)

    load_q.wait()
    split_rotation(0, 2 * C)
    for c in range(C):
        arrived(vext, 0, c)
        re, im = apply(vext, c)
        fext[c, 2 * N : 3 * N, 0:N] = (re / FILTER_HALF).astype(bf16)
        fext[c, 2 * N : 3 * N, N : 2 * N] = (im / FILTER_HALF).astype(bf16)
        send_own(fext, 1, c)
    split_rotation(2 * C, 4 * C)
    relay(fext, 1, (0, 1, 2), (0, 1, 2), (0, 1, 2))

    def y_copy(c, col):
        src, dst, kk = ((0, 1, k1), (0, 2, k2), (2, 3, k1))[col]
        return remote(yall.at[src, c], yall.at[dst, c], y_ss.at[c, col], y_rs.at[c, col], b, kk)

    def add_rotated(slot, c, kk):
        y = yall[slot, c]
        y_re, y_im = y[:, :N], y[:, N:]
        turned = jnp.concatenate(
            [jnp.concatenate([y_re, -y_im], axis=1), jnp.concatenate([y_im, y_re], axis=1)], axis=0
        )
        racc[...] = racc[...] + jnp.dot(turned, qv[kk * C + c], preferred_element_type=f32)

    racc[...] = jnp.zeros(racc.shape, f32)
    for c in range(C):
        arrived(fext, 1, c)
        re, im = apply(fext, c)
        anchor = vext[c, 2 * N : 3 * N, :].astype(f32)
        yall[0, c, :, 0:N] = (2.0 * re / FILTER_HALF - anchor[:, :N]).astype(bf16)
        yall[0, c, :, N : 2 * N] = (2.0 * im / FILTER_HALF - anchor[:, N:]).astype(bf16)
        y_copy(c, 1).start()
        y_copy(c, 0).start()
    for c in range(C):
        add_rotated(0, c, k)
    for c in range(C):
        y = yall[0, c]
        y_re, y_im = y[:, :N], y[:, N:]
        left = jnp.concatenate(
            [jnp.concatenate([y_re, y_im], axis=1), jnp.concatenate([-y_im, y_re], axis=1)], axis=0
        )
        left_t[c] = jnp.transpose(left)
    filt_copy = pltpu.make_async_copy(yall.at[0], filt_out, filt_sem.at[0])
    filt_copy.start()
    for c in range(C):
        y_copy(c, 0).wait_recv()
        add_rotated(1, c, k1)
    for c in range(C):
        y_copy(c, 1).wait_recv()
        y_copy(c, 2).start()
        add_rotated(2, c, k2)
    for c in range(C):
        y_copy(c, 2).wait_recv()
        add_rotated(3, c, k3)

    for i in range(NX):
        rr[i] = racc[:, i * N : (i + 1) * N].astype(bf16)
    def a_rows(step_y):
        return pl.ds(pl.multiple_of(lax.rem(yi + step_y, NY) * AR, 16), AR)

    def b_rows(step_y):
        return pl.ds(pl.multiple_of(NY * AR + lax.rem(yi + step_y, NY) * BR, 16), BR)

    def x_copy(d, j):
        i = lax.rem(xi + d, NX)
        return remote(
            wsend.at[i, a_rows(j), :], recvx.at[d - 1, a_rows(j), :], x_ss.at[d - 1, j], x_rs.at[d - 1, j], x_peer(d), k
        )

    def by_copy(d):
        return remote(wsend.at[:, b_rows(d), :], recvb.at[d - 1], by_ss.at[d - 1], by_rs.at[d - 1], y_peer(d), k)

    y_order = (2, 3, 1, 0)
    for d in (1, 3, 2, 0):
        i = lax.rem(xi + d, NX)
        panel = rr[i]
        for c in range(C):
            got = jnp.dot(left_t[c], panel, preferred_element_type=f32)
            for p in range(2):
                rows = slice(p * C * N + c * N, p * C * N + (c + 1) * N)
                wacc[i, rows, :] = got[p * N : (p + 1) * N]
                wsend[i, rows, :] = got[p * N : (p + 1) * N].astype(bf16)
        if d:
            for j in y_order:
                x_copy(d, j).start()
    for d in (2, 3, 1):
        by_copy(d).start()
    rot_copy = pltpu.make_async_copy(rr.at[k], rot_out, rot_sem.at[0])
    rot_copy.start()

    def y2_copy(d):
        return remote(xsb.at[d], recvy.at[d - 1], x2_ss.at[d - 1], x2_rs.at[d - 1], y_peer(d), k)

    def bx_copy(d):
        return remote(ysend.at[d], recvbx.at[d - 1], bx_ss.at[d - 1], bx_rs.at[d - 1], x_peer(d), k)

    def sum_a(j):
        for d in (1, 3, 2):
            x_copy(d, j).wait_recv()
        total = wacc[xi, a_rows(j), :]
        for d in range(NX - 1):
            total = total + recvx[d, a_rows(j), :].astype(f32)
        if j:
            xsb[j] = total.astype(bf16)
            y2_copy(j).start()
        else:
            xs[...] = total

    for j in y_order[:3]:
        sum_a(j)
    for d in (1, 3, 2):
        by_copy(d).wait_recv()
    for d in (1, 3, 2, 0):
        i = lax.rem(xi + d, NX)
        total = wacc[i, b_rows(0), :]
        for t in range(NY - 1):
            total = total + recvb[t, i].astype(f32)
        if d:
            ysend[d] = total.astype(bf16)
            bx_copy(d).start()
        else:
            ysb_own[...] = total
    sum_a(0)

    for d in range(1, NY):
        y2_copy(d).wait_recv()
    total = xs[...]
    for d in range(NY - 1):
        total = total + recvy[d].astype(f32)
    ys[0:AT] = total.reshape(AT, 16, N)
    ysb[0:AT] = total.astype(bf16).reshape(AT, 16, N)
    for d in range(1, NX):
        bx_copy(d).wait_recv()
    total = ysb_own[...]
    for d in range(NX - 1):
        total = total + recvbx[d].astype(f32)
    ys[AT:NZ] = total.reshape(NZ - AT, 16, N)
    ysb[AT:NZ] = total.astype(bf16).reshape(NZ - AT, 16, N)

    def z_copy(d):
        return remote(ysb.at[lax.rem(zi + d, NZ)], recvz.at[d - 1], z_ss.at[d - 1], z_rs.at[d - 1], z_peer(d), k)

    far_first = (6, 5, 7, 4, 8, 3, 9, 2, 10, 1, 11)
    for d in far_first:
        z_copy(d).start()
    for d in range(1, NZ):
        z_copy(d).wait_recv()
    total = ys[zi]
    for d in range(NZ - 1):
        total = total + recvz[d].astype(f32)
    inverse_root = 1.0 / jnp.sqrt(jnp.float32(N * BLOCKS))

    second = lax.div(zi, AT)
    start = (1 - second) * (yi * AR + zi * 16) + second * (NY * AR + yi * BR + (zi - AT) * 16)
    tile = pl.ds(pl.multiple_of(start, 16), 16)
    ag[xi, tile, :] = (total * inverse_root).astype(bf16)

    def az_copy(d):
        piece = ag.at[xi, tile, :]
        return remote(piece, piece, az_ss.at[d - 1], az_rs.at[d - 1], z_peer(d), k)

    for d in far_first:
        az_copy(d).start()
    for d in range(1, NZ):
        az_copy(d).wait_recv()

    def ay_copy(d):
        piece = ag.at[xi, a_rows(0), :]
        return remote(piece, piece, ay_ss.at[d - 1], ay_rs.at[d - 1], y_peer(d), k)

    def ax_copy(d, j):
        piece = ag.at[xi, a_rows(NY - j), :]
        return remote(piece, piece, ax_ss.at[d - 1, j], ax_rs.at[d - 1, j], x_peer(d), k)

    def cx_copy(d):
        piece = ag.at[xi, b_rows(0), :]
        return remote(piece, piece, cx_ss.at[d - 1], cx_rs.at[d - 1], x_peer(d), k)

    def cy_copy(d):
        piece = ag.at[:, b_rows(0), :]
        return remote(piece, piece, cy_ss.at[d - 1], cy_rs.at[d - 1], y_peer(d), k)

    for d in (1, 3, 2):
        cx_copy(d).start()
    for d in (2, 1, 3):
        ay_copy(d).start()
    for d in (1, 3, 2):
        ax_copy(d, 0).start()
    for d in (1, 3, 2):
        cx_copy(d).wait_recv()
    for d in (2, 3, 1):
        cy_copy(d).start()
    for j in (1, 3, 2):
        ay_copy(j).wait_recv()
        for d in (1, 3, 2):
            ax_copy(d, j).start()
    for d in (1, 3, 2):
        cy_copy(d).wait_recv()

    inter_copies = []
    for d in (0, 1, 3, 2):
        if d:
            for j in range(NY):
                ax_copy(d, j).wait_recv()
        i = lax.rem(xi + (NX - d), NX)
        inter_copies.append(pltpu.make_async_copy(ag.at[i], inter_out.at[i], inter_sem.at[d]))
        inter_copies[-1].start()

    @pl.when(has_right)
    def _():
        pk_right.wait_send()

    @pl.when(has_left)
    def _():
        pk_left.wait_send()

    for rnd, buf in ((0, vext), (1, fext)):
        for c in range(C):
            @pl.when(has_right)
            def _():
                hop(buf, rnd, c, 0).wait_send()

            @pl.when(has_left)
            def _():
                hop(buf, rnd, c, 1).wait_send()

            @pl.when(inner)
            def _():
                hop(buf, rnd, c, 2).wait_send()
                hop(buf, rnd, c, 3).wait_send()

    for c in range(C):
        for col in range(3):
            y_copy(c, col).wait_send()
    for d in range(1, NX):
        for j in range(NY):
            x_copy(d, j).wait_send()
            ax_copy(d, j).wait_send()
        bx_copy(d).wait_send()
        cx_copy(d).wait_send()
    for d in range(1, NY):
        y2_copy(d).wait_send()
        ay_copy(d).wait_send()
        by_copy(d).wait_send()
        cy_copy(d).wait_send()
    for d in range(1, NZ):
        z_copy(d).wait_send()
        az_copy(d).wait_send()
    for copy in [filt_copy, rot_copy] + inter_copies:
        copy.wait()


def write_out(filt, rot, inter, filt_out, rot_out, inter_out, filt_v, rot_v, inter_v, filt_f, rot_f, inter_f, in_sem, out_sem):
    reads = [pltpu.make_async_copy(filt, filt_v, in_sem.at[0]), pltpu.make_async_copy(rot, rot_v, in_sem.at[1])]
    reads += [pltpu.make_async_copy(inter.at[i], inter_v.at[i], in_sem.at[2 + i]) for i in range(NX)]
    writes = [pltpu.make_async_copy(filt_f, filt_out, out_sem.at[0]), pltpu.make_async_copy(rot_f, rot_out, out_sem.at[1])]
    for read in reads[2:] + reads[:2]:
        read.start()
    for i in range(NX):
        reads[2 + i].wait()
        inter_f[i] = inter_v[i].astype(jnp.float32)
        for p in range(2):
            writes.append(
                pltpu.make_async_copy(
                    inter_f.at[i, pl.ds(p * C * N, C * N), :],
                    inter_out.at[:, p, pl.ds(i * N, N)],
                    out_sem.at[2 + 2 * i + p],
                )
            )
            writes[-1].start()
    reads[0].wait()
    for c in range(C):
        y = filt_v[c]
        filt_f[:, :, c * N : (c + 1) * N] = jnp.swapaxes(jnp.stack([y[:, :N], y[:, N:]], axis=0), 0, 1)
    writes[0].start()
    reads[1].wait()
    rot_f[...] = jnp.swapaxes(rot_v[...].reshape(2, N, N), 0, 1)
    writes[1].start()
    for write in writes:
        write.wait()


def on_device(orbitals, elem_count, connectivity, elem_coef, elem_matrix, potential, absorber, rotation):
    f32, bf16 = jnp.float32, jnp.bfloat16
    anywhere = pl.BlockSpec(memory_space=pl.ANY)
    dma = pltpu.SemaphoreType.DMA
    results = pl.pallas_call(
        body,
        out_shape=(
            jax.ShapeDtypeStruct((C, N, 2 * N), bf16),
            jax.ShapeDtypeStruct((2 * N, N), bf16),
            jax.ShapeDtypeStruct((NX, 6 * N, N), bf16),
        ),
        in_specs=[anywhere] * 8,
        out_specs=(anywhere, anywhere, anywhere),
        scratch_shapes=[
            pltpu.VMEM(connectivity.shape, jnp.int32),
            pltpu.VMEM(elem_coef.shape, f32),
            pltpu.SMEM((1,), jnp.int32),
            pltpu.VMEM(elem_matrix.shape, bf16),
            pltpu.VMEM((1, N), f32),
            pltpu.VMEM((1, N), f32),
            pltpu.VMEM((3, 8, JP), f32),
            pltpu.VMEM((JP, JP), bf16),
            pltpu.VMEM((2, N, N), f32),
            pltpu.VMEM((4 * JP, JP), bf16),
            pltpu.VMEM((4 * N, JP), bf16),
            pltpu.VMEM((2 * N, 4 * JP), bf16),
            pltpu.VMEM((N, 5 * N), f32),
            pltpu.VMEM((2 * N, 5 * N), bf16),
            pltpu.VMEM((N, 2, C * N), bf16),
            pltpu.VMEM((C, 5 * N, 2 * N), bf16),
            pltpu.VMEM((C, 5 * N, 2 * N), bf16),
            pltpu.VMEM((4 * C * N, 2, 4 * N), bf16),
            pltpu.VMEM((4 * C, 2 * N, 4 * N), bf16),
            pltpu.VMEM((4, C, N, 2 * N), bf16),
            pltpu.VMEM((C, 2 * N, 2 * N), bf16),
            pltpu.VMEM((2 * N, 4 * N), f32),
            pltpu.VMEM((4, 2 * N, N), bf16),
            pltpu.VMEM((NX, 6 * N, N), f32),
            pltpu.VMEM((NX, 6 * N, N), bf16),
            pltpu.VMEM((NX - 1, NY * AR, N), bf16),
            pltpu.VMEM((AR, N), f32),
            pltpu.VMEM((NY, AR, N), bf16),
            pltpu.VMEM((NY - 1, AR, N), bf16),
            pltpu.VMEM((NY - 1, NX, BR, N), bf16),
            pltpu.VMEM((NX, BR, N), bf16),
            pltpu.VMEM((BR, N), f32),
            pltpu.VMEM((NX - 1, BR, N), bf16),
            pltpu.VMEM((NZ, 16, N), f32),
            pltpu.VMEM((NZ, 16, N), bf16),
            pltpu.VMEM((NZ - 1, 16, N), bf16),
            pltpu.VMEM((NX, 6 * N, N), bf16),
            dma((6,)), dma((1,)), dma((1,)), dma((1,)), dma((1,)), dma((NX,)),
            dma((2,)), dma((2,)),
            dma((2, C, 4)), dma((2, C, 4)),
            dma((C, 3)), dma((C, 3)),
            dma((NX - 1, NY)), dma((NX - 1, NY)),
            dma((NY - 1,)), dma((NY - 1,)),
            dma((NZ - 1,)), dma((NZ - 1,)),
            dma((NZ - 1,)), dma((NZ - 1,)),
            dma((NY - 1,)), dma((NY - 1,)),
            dma((NX - 1, NY)), dma((NX - 1, NY)),
            dma((NY - 1,)), dma((NY - 1,)),
            dma((NX - 1,)), dma((NX - 1,)),
            dma((NX - 1,)), dma((NX - 1,)),
            dma((NY - 1,)), dma((NY - 1,)),
        ],
        compiler_params=pltpu.CompilerParams(collective_id=0, has_side_effects=True, vmem_limit_bytes=VMEM_LIMIT),
        name="filter_panel",
    )(
        orbitals, connectivity, elem_coef, elem_count, elem_matrix,
        potential.reshape(1, N), absorber.reshape(1, N), rotation,
    )
    outs = ((N, 2, C * N), (N, 2, N), (C * N, 2, NX * N))
    return pl.pallas_call(
        write_out,
        out_shape=tuple(jax.ShapeDtypeStruct(shape, kind) for shape, kind in zip(outs, (bf16, bf16, f32))),
        in_specs=[anywhere] * 3,
        out_specs=(anywhere,) * 3,
        scratch_shapes=[pltpu.VMEM(r.shape, r.dtype) for r in results]
        + [pltpu.VMEM(outs[0], bf16), pltpu.VMEM(outs[1], bf16), pltpu.VMEM((NX, 6 * N, N), f32), dma((6,)), dma((10,))],
        compiler_params=pltpu.CompilerParams(vmem_limit_bytes=VMEM_LIMIT),
        name="write_out",
    )(*results)


def solution(mesh):
    placed = (
        P("elem", None, "band"),
        P("elem"),
        P("elem", None, None),
        P("elem", None),
        P(),
        P("elem"),
        P("elem"),
        P(),
    )
    return jax.shard_map(
        on_device,
        mesh=mesh,
        in_specs=placed,
        out_specs=(P("elem", None, "band"), P("elem", None, "band"), P("band", None, None)),
        check_vma=False,
    )
```

```python
import functools

import jax
import jax.numpy as jnp
from jax import lax
from jax.experimental import pallas as pl
from jax.experimental.pallas import tpu as pltpu
from jax.sharding import PartitionSpec as P

MESH = pl.DeviceIdType.MESH
FILTER_CENTER = 1.0
FILTER_HALF = 4.0

N = 128
C = 3
NX, NY, NZ = 4, 4, 12
BLOCKS = NX * NY * NZ
JP = 384
VMEM_LIMIT = 66500000
AT = 9
AR = AT * 16
BR = (NZ - AT) * 16
PREV, OWN, NEXT = 0, 1, 2


def body(
    orb, ids_hbm, coef_hbm, count_hbm, mat_hbm, pot_hbm, cap_hbm, rot, filt_out, rot_out, inter_out,
    ids_in, coef_in, count_in, mat_in, pot_in, cap_in, pk, mat, diag, gall, gmine, both, sacc, s2, orb_raw, vext, fext, q_raw, qv, yall, left_t, racc, rr, wacc, wsend, recvx, xs, xsb,
    recvy, recvb, ysend, ysb_own, recvbx, ys, ysb, recvz, ag,
    small_sem, orb_sem, q_sem, filt_sem, rot_sem, inter_sem, pk_ss, pk_rs, h_ss, h_rs, y_ss, y_rs, x_ss, x_rs,
    x2_ss, x2_rs, z_ss, z_rs, az_ss, az_rs, ay_ss, ay_rs, ax_ss, ax_rs,
    by_ss, by_rs, bx_ss, bx_rs, cx_ss, cx_rs, cy_ss, cy_rs,
):
    f32, bf16 = jnp.float32, jnp.bfloat16
    b = lax.axis_index("elem")
    k = lax.axis_index("band")
    xi = lax.rem(b, NX)
    yi = lax.rem(lax.div(b, NX), NY)
    zi = lax.div(b, NX * NY)
    k1 = k + 1 - 2 * lax.rem(k, 2)
    k2 = lax.rem(k + 2, 4)
    k3 = 3 - k
    has_left = b > 0
    has_right = b < BLOCKS - 1
    inner = has_left & has_right
    place = lax.rem(b, NX * NY)

    def x_peer(d):
        return b - xi + lax.rem(xi + d, NX)

    def y_peer(d):
        return b + (lax.rem(yi + d, NY) - yi) * NX

    def z_peer(d):
        return b + (lax.rem(zi + d, NZ) - zi) * (NX * NY)

    barrier = pltpu.get_barrier_semaphore()

    def greet(e, kk):
        pl.semaphore_signal(barrier, inc=1, device_id=(e, kk), device_id_type=MESH)

    for d in range(1, NZ):
        greet(z_peer(d), k)

    @pl.when(has_left)
    def _():
        greet(b - 1, k)

    @pl.when(has_right)
    def _():
        greet(b + 1, k)

    greet(b, k2)
    for d in range(1, NY):
        greet(y_peer(d), k)
    for d in range(1, NX):
        greet(x_peer(d), k)
    greet(b, k1)

    load_orb = pltpu.make_async_copy(orb, orb_raw, orb_sem.at[0])
    load_orb.start()
    smalls = [
        pltpu.make_async_copy(src, dst, small_sem.at[i])
        for i, (src, dst) in enumerate(
            ((ids_hbm, ids_in), (coef_hbm, coef_in), (count_hbm, count_in), (pot_hbm, pot_in), (cap_hbm, cap_in), (mat_hbm, mat_in))
        )
    ]
    for load in smalls:
        load.start()
    load_q = pltpu.make_async_copy(rot, q_raw, q_sem.at[0])
    load_q.start()

    def clear(slot):
        zeros = jnp.zeros((C, N, 2 * N), bf16)
        vext[:, slot * N : (slot + 1) * N, :] = zeros
        fext[:, slot * N : (slot + 1) * N, :] = zeros

    @pl.when(b < 2)
    def _():
        clear(0)

    @pl.when(b < 1)
    def _():
        clear(1)
        pk[PREV] = jnp.zeros(pk.shape[1:], f32)

    @pl.when(b > BLOCKS - 3)
    def _():
        clear(4)

    @pl.when(b > BLOCKS - 2)
    def _():
        clear(3)
        pk[NEXT] = jnp.zeros(pk.shape[1:], f32)

    nodes = mat_in.shape[0]
    for load in smalls[:3]:
        load.wait()
    pk[OWN] = jnp.full(pk.shape[1:], -1.0, f32)
    pk[OWN, 0:4, 0:nodes] = ids_in[0].astype(f32)
    live = jnp.where(lax.broadcasted_iota(jnp.int32, (1, 4), 1) < count_in[0], coef_in[...], 0.0)
    for e in range(4):
        pk[OWN, 4 + e : 5 + e, :] = jnp.broadcast_to(live[:, e : e + 1], (1, JP))

    load_orb.wait()
    planes = jnp.swapaxes(orb_raw[...], 0, 1)
    for c in range(C):
        for p in range(2):
            vext[c, 2 * N : 3 * N, p * N : (p + 1) * N] = planes[p, :, c * N : (c + 1) * N]
    beside = sum(side.astype(jnp.int32) for side in (has_left, has_right))
    pl.semaphore_wait(barrier, 2 + NX - 1 + NY - 1 + NZ - 1 + beside)

    def remote(src, dst, ss, rs, e, kk):
        return pltpu.make_async_remote_copy(
            src_ref=src, dst_ref=dst, send_sem=ss, recv_sem=rs, device_id=(e, kk), device_id_type=MESH
        )

    def hop(buf, rnd, c, col):
        src_slot, dst_slot, step = ((2, 1, 1), (2, 3, -1), (1, 0, 1), (3, 4, -1))[col]
        return remote(
            buf.at[c, pl.ds(src_slot * N, N), :],
            buf.at[c, pl.ds(dst_slot * N, N), :],
            h_ss.at[rnd, c, col],
            h_rs.at[rnd, c, col],
            b + step,
            k,
        )

    pk_right = remote(pk.at[OWN], pk.at[PREV], pk_ss.at[0], pk_rs.at[0], b + 1, k)
    pk_left = remote(pk.at[OWN], pk.at[NEXT], pk_ss.at[1], pk_rs.at[1], b - 1, k)

    @pl.when(has_right)
    def _():
        pk_right.start()

    @pl.when(has_left)
    def _():
        pk_left.start()

    def send_own(buf, rnd, c):
        @pl.when(has_right)
        def _():
            hop(buf, rnd, c, 0).start()

        @pl.when(has_left)
        def _():
            hop(buf, rnd, c, 1).start()

    def from_left(buf, rnd, c):
        @pl.when(has_left)
        def _():
            hop(buf, rnd, c, 0).wait_recv()

        @pl.when(inner)
        def _():
            hop(buf, rnd, c, 2).start()

    def from_right(buf, rnd, c):
        @pl.when(has_right)
        def _():
            hop(buf, rnd, c, 1).wait_recv()

        @pl.when(inner)
        def _():
            hop(buf, rnd, c, 3).start()

    def relay(buf, rnd, near, even, far):
        @pl.when(place == 0)
        def _():
            for c in near:
                from_right(buf, rnd, c)
            for c in far:
                from_left(buf, rnd, c)

        @pl.when(place == NX * NY - 1)
        def _():
            for c in near:
                from_left(buf, rnd, c)
            for c in far:
                from_right(buf, rnd, c)

        @pl.when((place > 0) & (place < NX * NY - 1))
        def _():
            for c in even:
                from_left(buf, rnd, c)
                from_right(buf, rnd, c)

    def arrived(buf, rnd, c):
        @pl.when(b > 1)
        def _():
            hop(buf, rnd, c, 2).wait_recv()

        @pl.when(b < BLOCKS - 2)
        def _():
            hop(buf, rnd, c, 3).wait_recv()

    for c in range(C):
        send_own(vext, 0, c)

    for load in smalls[3:]:
        load.wait()
    mat[...] = jnp.zeros(mat.shape, bf16)
    mat[0:nodes, 0:nodes] = mat_in[...]
    diag[0] = jnp.transpose(jnp.broadcast_to(pot_in[...], (N, N)))
    diag[1] = jnp.transpose(jnp.broadcast_to(cap_in[...], (N, N)))
    sacc[...] = jnp.zeros(sacc.shape, f32)

    def add_strip(which):
        rows = pk[which]
        columns = jnp.transpose(rows)
        lanes = lax.broadcasted_iota(jnp.int32, (JP, JP), 1).astype(f32)
        mine = (lax.broadcasted_iota(jnp.int32, (N, JP), 0) + (2 - which) * N).astype(f32)
        for e in range(4):
            gall[e * JP : (e + 1) * JP, :] = jnp.where(lanes == columns[:, e : e + 1], 1.0, 0.0).astype(bf16)
            gmine[e * N : (e + 1) * N, :] = jnp.where(mine == rows[e : e + 1, :], 1.0, 0.0).astype(bf16)
        part = jnp.dot(gmine[...], mat[...], preferred_element_type=f32)
        for e in range(4):
            term = part[e * N : (e + 1) * N] * rows[4 + e : 5 + e, :]
            high = term.astype(bf16)
            both[0:N, e * JP : (e + 1) * JP] = high
            both[N : 2 * N, e * JP : (e + 1) * JP] = (term - high.astype(f32)).astype(bf16)
        got = jnp.dot(both[...], gall[...], preferred_element_type=f32)
        cols = pl.ds(pl.multiple_of(which * N, N), JP)
        sacc[:, cols] = sacc[:, cols] + got[:N] + got[N:]

    def pack_from_left():
        @pl.when(has_left)
        def _():
            pk_right.wait_recv()

    def pack_from_right():
        @pl.when(has_right)
        def _():
            pk_left.wait_recv()

    add_strip(OWN)
    relay(vext, 0, (0, 1), (0,), ())
    right_first = place == 0

    @pl.when(right_first)
    def _():
        pack_from_right()

    @pl.when(place > 0)
    def _():
        pack_from_left()

    step = right_first.astype(jnp.int32)
    add_strip(2 * step)
    relay(vext, 0, (2,), (1, 2), (0, 1, 2))

    @pl.when(right_first)
    def _():
        pack_from_left()

    @pl.when(place > 0)
    def _():
        pack_from_right()

    add_strip(2 - 2 * step)

    high = sacc[...].astype(bf16)
    s2[0:N, :] = high
    s2[N : 2 * N, :] = (sacc[...] - high.astype(f32)).astype(bf16)

    def apply(buf, c):
        two = jnp.dot(s2[...], buf[c], preferred_element_type=f32)
        k_v = two[:N] + two[N:]
        own = buf[c, 2 * N : 3 * N, :].astype(f32)
        v_re, v_im = own[:, :N], own[:, N:]
        ham_re = k_v[:, :N] + diag[0] * v_re + diag[1] * v_im
        ham_im = k_v[:, N:] + diag[0] * v_im - diag[1] * v_re
        return (ham_re - FILTER_CENTER * v_re), (ham_im - FILTER_CENTER * v_im)

    def split_rotation(first, last):
        def one(i, carry):
            planes = jnp.swapaxes(q_raw[pl.ds(pl.multiple_of(i * N, N), N)], 0, 1)
            qv[i, 0:N, :] = planes[0]
            qv[i, N : 2 * N, :] = planes[1]
            return carry

        lax.fori_loop(first, last, one, 0)

    for c in range(C):
        arrived(vext, 0, c)
        re, im = apply(vext, c)
        fext[c, 2 * N : 3 * N, 0:N] = (re / FILTER_HALF).astype(bf16)
        fext[c, 2 * N : 3 * N, N : 2 * N] = (im / FILTER_HALF).astype(bf16)
        send_own(fext, 1, c)
    relay(fext, 1, (0, 1, 2), (0, 1, 2), (0, 1, 2))

    def y_copy(c, col):
        src, dst, kk = ((0, 1, k1), (0, 2, k2), (2, 3, k1))[col]
        return remote(yall.at[src, c], yall.at[dst, c], y_ss.at[c, col], y_rs.at[c, col], b, kk)

    def add_rotated(slot, c, kk):
        y = yall[slot, c]
        y_re, y_im = y[:, :N], y[:, N:]
        turned = jnp.concatenate(
            [jnp.concatenate([y_re, -y_im], axis=1), jnp.concatenate([y_im, y_re], axis=1)], axis=0
        )
        racc[...] = racc[...] + jnp.dot(turned, qv[kk * C + c], preferred_element_type=f32)

    racc[...] = jnp.zeros(racc.shape, f32)
    for c in range(C):
        arrived(fext, 1, c)
        re, im = apply(fext, c)
        anchor = vext[c, 2 * N : 3 * N, :].astype(f32)
        yall[0, c, :, 0:N] = (2.0 * re / FILTER_HALF - anchor[:, :N]).astype(bf16)
        yall[0, c, :, N : 2 * N] = (2.0 * im / FILTER_HALF - anchor[:, N:]).astype(bf16)
        y_copy(c, 1).start()
        y_copy(c, 0).start()
    load_q.wait()
    split_rotation(0, 4 * C)
    for c in range(C):
        add_rotated(0, c, k)
    for c in range(C):
        y = yall[0, c]
        y_re, y_im = y[:, :N], y[:, N:]
        left = jnp.concatenate(
            [jnp.concatenate([y_re, y_im], axis=1), jnp.concatenate([-y_im, y_re], axis=1)], axis=0
        )
        left_t[c] = jnp.transpose(left)
    filt_copy = pltpu.make_async_copy(yall.at[0], filt_out, filt_sem.at[0])
    filt_copy.start()
    for c in range(C):
        y_copy(c, 0).wait_recv()
        add_rotated(1, c, k1)
    for c in range(C):
        y_copy(c, 1).wait_recv()
        y_copy(c, 2).start()
        add_rotated(2, c, k2)
    for c in range(C):
        y_copy(c, 2).wait_recv()
        add_rotated(3, c, k3)

    for i in range(NX):
        rr[i] = racc[:, i * N : (i + 1) * N].astype(bf16)
    def a_rows(step_y):
        return pl.ds(pl.multiple_of(lax.rem(yi + step_y, NY) * AR, 16), AR)

    def b_rows(step_y):
        return pl.ds(pl.multiple_of(NY * AR + lax.rem(yi + step_y, NY) * BR, 16), BR)

    def x_copy(d, j):
        i = lax.rem(xi + d, NX)
        return remote(
            wsend.at[i, a_rows(j), :], recvx.at[d - 1, a_rows(j), :], x_ss.at[d - 1, j], x_rs.at[d - 1, j], x_peer(d), k
        )

    def by_copy(d):
        return remote(wsend.at[:, b_rows(d), :], recvb.at[d - 1], by_ss.at[d - 1], by_rs.at[d - 1], y_peer(d), k)

    y_order = (2, 3, 1, 0)
    for d in (1, 3, 2, 0):
        i = lax.rem(xi + d, NX)
        panel = rr[i]
        for c in range(C):
            got = jnp.dot(left_t[c], panel, preferred_element_type=f32)
            for p in range(2):
                rows = slice(p * C * N + c * N, p * C * N + (c + 1) * N)
                wacc[i, rows, :] = got[p * N : (p + 1) * N]
                wsend[i, rows, :] = got[p * N : (p + 1) * N].astype(bf16)
        if d:
            for j in y_order:
                x_copy(d, j).start()
    for d in (2, 3, 1):
        by_copy(d).start()
    rot_copy = pltpu.make_async_copy(rr.at[k], rot_out, rot_sem.at[0])
    rot_copy.start()

    def y2_copy(d):
        return remote(xsb.at[d], recvy.at[d - 1], x2_ss.at[d - 1], x2_rs.at[d - 1], y_peer(d), k)

    def bx_copy(d):
        return remote(ysend.at[d], recvbx.at[d - 1], bx_ss.at[d - 1], bx_rs.at[d - 1], x_peer(d), k)

    def sum_a(j):
        for d in (1, 3, 2):
            x_copy(d, j).wait_recv()
        total = wacc[xi, a_rows(j), :]
        for d in range(NX - 1):
            total = total + recvx[d, a_rows(j), :].astype(f32)
        if j:
            xsb[j] = total.astype(bf16)
            y2_copy(j).start()
        else:
            xs[...] = total

    for j in y_order[:3]:
        sum_a(j)
    for d in (1, 3, 2):
        by_copy(d).wait_recv()
    for d in (1, 3, 2, 0):
        i = lax.rem(xi + d, NX)
        total = wacc[i, b_rows(0), :]
        for t in range(NY - 1):
            total = total + recvb[t, i].astype(f32)
        if d:
            ysend[d] = total.astype(bf16)
            bx_copy(d).start()
        else:
            ysb_own[...] = total
    sum_a(0)

    for d in range(1, NY):
        y2_copy(d).wait_recv()
    total = xs[...]
    for d in range(NY - 1):
        total = total + recvy[d].astype(f32)
    ys[0:AT] = total.reshape(AT, 16, N)
    ysb[0:AT] = total.astype(bf16).reshape(AT, 16, N)
    for d in range(1, NX):
        bx_copy(d).wait_recv()
    total = ysb_own[...]
    for d in range(NX - 1):
        total = total + recvbx[d].astype(f32)
    ys[AT:NZ] = total.reshape(NZ - AT, 16, N)
    ysb[AT:NZ] = total.astype(bf16).reshape(NZ - AT, 16, N)

    def z_copy(d):
        return remote(ysb.at[lax.rem(zi + d, NZ)], recvz.at[d - 1], z_ss.at[d - 1], z_rs.at[d - 1], z_peer(d), k)

    far_first = (6, 5, 7, 4, 8, 3, 9, 2, 10, 1, 11)
    for d in far_first:
        z_copy(d).start()
    for d in range(1, NZ):
        z_copy(d).wait_recv()
    total = ys[zi]
    for d in range(NZ - 1):
        total = total + recvz[d].astype(f32)
    inverse_root = 1.0 / jnp.sqrt(jnp.float32(N * BLOCKS))

    second = lax.div(zi, AT)
    start = (1 - second) * (yi * AR + zi * 16) + second * (NY * AR + yi * BR + (zi - AT) * 16)
    tile = pl.ds(pl.multiple_of(start, 16), 16)
    ag[xi, tile, :] = (total * inverse_root).astype(bf16)

    def az_copy(d):
        piece = ag.at[xi, tile, :]
        return remote(piece, piece, az_ss.at[d - 1], az_rs.at[d - 1], z_peer(d), k)

    for d in far_first:
        az_copy(d).start()
    for d in range(1, NZ):
        az_copy(d).wait_recv()

    def ay_copy(d):
        piece = ag.at[xi, a_rows(0), :]
        return remote(piece, piece, ay_ss.at[d - 1], ay_rs.at[d - 1], y_peer(d), k)

    def ax_copy(d, j):
        piece = ag.at[xi, a_rows(NY - j), :]
        return remote(piece, piece, ax_ss.at[d - 1, j], ax_rs.at[d - 1, j], x_peer(d), k)

    def cx_copy(d):
        piece = ag.at[xi, b_rows(0), :]
        return remote(piece, piece, cx_ss.at[d - 1], cx_rs.at[d - 1], x_peer(d), k)

    def cy_copy(d):
        piece = ag.at[:, b_rows(0), :]
        return remote(piece, piece, cy_ss.at[d - 1], cy_rs.at[d - 1], y_peer(d), k)

    for d in (1, 3, 2):
        cx_copy(d).start()
    for d in (2, 1, 3):
        ay_copy(d).start()
    for d in (1, 3, 2):
        ax_copy(d, 0).start()
    for d in (1, 3, 2):
        cx_copy(d).wait_recv()
    for d in (2, 3, 1):
        cy_copy(d).start()
    for j in (1, 3, 2):
        ay_copy(j).wait_recv()
        for d in (1, 3, 2):
            ax_copy(d, j).start()
    for d in (1, 3, 2):
        cy_copy(d).wait_recv()

    inter_copies = []
    for d in (0, 1, 3, 2):
        if d:
            for j in range(NY):
                ax_copy(d, j).wait_recv()
        i = lax.rem(xi + (NX - d), NX)
        inter_copies.append(pltpu.make_async_copy(ag.at[i], inter_out.at[i], inter_sem.at[d]))
        inter_copies[-1].start()

    @pl.when(has_right)
    def _():
        pk_right.wait_send()

    @pl.when(has_left)
    def _():
        pk_left.wait_send()

    for rnd, buf in ((0, vext), (1, fext)):
        for c in range(C):
            @pl.when(has_right)
            def _():
                hop(buf, rnd, c, 0).wait_send()

            @pl.when(has_left)
            def _():
                hop(buf, rnd, c, 1).wait_send()

            @pl.when(inner)
            def _():
                hop(buf, rnd, c, 2).wait_send()
                hop(buf, rnd, c, 3).wait_send()

    for c in range(C):
        for col in range(3):
            y_copy(c, col).wait_send()
    for d in range(1, NX):
        for j in range(NY):
            x_copy(d, j).wait_send()
            ax_copy(d, j).wait_send()
        bx_copy(d).wait_send()
        cx_copy(d).wait_send()
    for d in range(1, NY):
        y2_copy(d).wait_send()
        ay_copy(d).wait_send()
        by_copy(d).wait_send()
        cy_copy(d).wait_send()
    for d in range(1, NZ):
        z_copy(d).wait_send()
        az_copy(d).wait_send()
    for copy in [filt_copy, rot_copy] + inter_copies:
        copy.wait()


def write_out(filt, rot, inter, filt_out, rot_out, inter_out, filt_v, rot_v, inter_v, filt_f, rot_f, inter_f, in_sem, out_sem):
    reads = [pltpu.make_async_copy(filt, filt_v, in_sem.at[0]), pltpu.make_async_copy(rot, rot_v, in_sem.at[1])]
    reads += [pltpu.make_async_copy(inter.at[i], inter_v.at[i], in_sem.at[2 + i]) for i in range(NX)]
    writes = [pltpu.make_async_copy(filt_f, filt_out, out_sem.at[0]), pltpu.make_async_copy(rot_f, rot_out, out_sem.at[1])]
    for read in reads[2:] + reads[:2]:
        read.start()
    for i in range(NX):
        reads[2 + i].wait()
        inter_f[i] = inter_v[i].astype(jnp.float32)
        for p in range(2):
            writes.append(
                pltpu.make_async_copy(
                    inter_f.at[i, pl.ds(p * C * N, C * N), :],
                    inter_out.at[:, p, pl.ds(i * N, N)],
                    out_sem.at[2 + 2 * i + p],
                )
            )
            writes[-1].start()
    reads[0].wait()
    for c in range(C):
        y = filt_v[c]
        filt_f[:, :, c * N : (c + 1) * N] = jnp.swapaxes(jnp.stack([y[:, :N], y[:, N:]], axis=0), 0, 1)
    writes[0].start()
    reads[1].wait()
    rot_f[...] = jnp.swapaxes(rot_v[...].reshape(2, N, N), 0, 1)
    writes[1].start()
    for write in writes:
        write.wait()


def on_device(orbitals, elem_count, connectivity, elem_coef, elem_matrix, potential, absorber, rotation):
    f32, bf16 = jnp.float32, jnp.bfloat16
    anywhere = pl.BlockSpec(memory_space=pl.ANY)
    dma = pltpu.SemaphoreType.DMA
    results = pl.pallas_call(
        body,
        out_shape=(
            jax.ShapeDtypeStruct((C, N, 2 * N), bf16),
            jax.ShapeDtypeStruct((2 * N, N), bf16),
            jax.ShapeDtypeStruct((NX, 6 * N, N), bf16),
        ),
        in_specs=[anywhere] * 8,
        out_specs=(anywhere, anywhere, anywhere),
        scratch_shapes=[
            pltpu.VMEM(connectivity.shape, jnp.int32),
            pltpu.VMEM(elem_coef.shape, f32),
            pltpu.SMEM((1,), jnp.int32),
            pltpu.VMEM(elem_matrix.shape, bf16),
            pltpu.VMEM((1, N), f32),
            pltpu.VMEM((1, N), f32),
            pltpu.VMEM((3, 8, JP), f32),
            pltpu.VMEM((JP, JP), bf16),
            pltpu.VMEM((2, N, N), f32),
            pltpu.VMEM((4 * JP, JP), bf16),
            pltpu.VMEM((4 * N, JP), bf16),
            pltpu.VMEM((2 * N, 4 * JP), bf16),
            pltpu.VMEM((N, 5 * N), f32),
            pltpu.VMEM((2 * N, 5 * N), bf16),
            pltpu.VMEM((N, 2, C * N), bf16),
            pltpu.VMEM((C, 5 * N, 2 * N), bf16),
            pltpu.VMEM((C, 5 * N, 2 * N), bf16),
            pltpu.VMEM((4 * C * N, 2, 4 * N), bf16),
            pltpu.VMEM((4 * C, 2 * N, 4 * N), bf16),
            pltpu.VMEM((4, C, N, 2 * N), bf16),
            pltpu.VMEM((C, 2 * N, 2 * N), bf16),
            pltpu.VMEM((2 * N, 4 * N), f32),
            pltpu.VMEM((4, 2 * N, N), bf16),
            pltpu.VMEM((NX, 6 * N, N), f32),
            pltpu.VMEM((NX, 6 * N, N), bf16),
            pltpu.VMEM((NX - 1, NY * AR, N), bf16),
            pltpu.VMEM((AR, N), f32),
            pltpu.VMEM((NY, AR, N), bf16),
            pltpu.VMEM((NY - 1, AR, N), bf16),
            pltpu.VMEM((NY - 1, NX, BR, N), bf16),
            pltpu.VMEM((NX, BR, N), bf16),
            pltpu.VMEM((BR, N), f32),
            pltpu.VMEM((NX - 1, BR, N), bf16),
            pltpu.VMEM((NZ, 16, N), f32),
            pltpu.VMEM((NZ, 16, N), bf16),
            pltpu.VMEM((NZ - 1, 16, N), bf16),
            pltpu.VMEM((NX, 6 * N, N), bf16),
            dma((6,)), dma((1,)), dma((1,)), dma((1,)), dma((1,)), dma((NX,)),
            dma((2,)), dma((2,)),
            dma((2, C, 4)), dma((2, C, 4)),
            dma((C, 3)), dma((C, 3)),
            dma((NX - 1, NY)), dma((NX - 1, NY)),
            dma((NY - 1,)), dma((NY - 1,)),
            dma((NZ - 1,)), dma((NZ - 1,)),
            dma((NZ - 1,)), dma((NZ - 1,)),
            dma((NY - 1,)), dma((NY - 1,)),
            dma((NX - 1, NY)), dma((NX - 1, NY)),
            dma((NY - 1,)), dma((NY - 1,)),
            dma((NX - 1,)), dma((NX - 1,)),
            dma((NX - 1,)), dma((NX - 1,)),
            dma((NY - 1,)), dma((NY - 1,)),
        ],
        compiler_params=pltpu.CompilerParams(collective_id=0, has_side_effects=True, vmem_limit_bytes=VMEM_LIMIT),
        name="filter_panel",
    )(
        orbitals, connectivity, elem_coef, elem_count, elem_matrix,
        potential.reshape(1, N), absorber.reshape(1, N), rotation,
    )
    outs = ((N, 2, C * N), (N, 2, N), (C * N, 2, NX * N))
    return pl.pallas_call(
        write_out,
        out_shape=tuple(jax.ShapeDtypeStruct(shape, kind) for shape, kind in zip(outs, (bf16, bf16, f32))),
        in_specs=[anywhere] * 3,
        out_specs=(anywhere,) * 3,
        scratch_shapes=[pltpu.VMEM(r.shape, r.dtype) for r in results]
        + [pltpu.VMEM(outs[0], bf16), pltpu.VMEM(outs[1], bf16), pltpu.VMEM((NX, 6 * N, N), f32), dma((6,)), dma((10,))],
        compiler_params=pltpu.CompilerParams(vmem_limit_bytes=VMEM_LIMIT),
        name="write_out",
    )(*results)


def solution(mesh):
    placed = (
        P("elem", None, "band"),
        P("elem"),
        P("elem", None, None),
        P("elem", None),
        P(),
        P("elem"),
        P("elem"),
        P(),
    )
    return jax.shard_map(
        on_device,
        mesh=mesh,
        in_specs=placed,
        out_specs=(P("elem", None, "band"), P("elem", None, "band"), P("band", None, None)),
        check_vma=False,
    )
```
